256 devices in a mesh: nodes: 32 (over y, x, core), queries: 8 (over z).
Axes of the slice: x: 4, y: 4, z: 8, core: 2. Of those that a mesh axis runs over, the one named last changes fastest.
Arguments:
- state_in: float32 [8192, 1024], P('nodes', 'queries')
- edge_src: int32 [131072], P('nodes'), may hold values from 0 to 2303
- edge_dst: int32 [131072], P('nodes'), may hold values from 0 to 255
- edge_rel: int32 [131072], P('nodes'), may hold values from 0 to 534
- edge_count: int32 [32], P('nodes'), may hold values from 1024 to 4096, as said below
- send_list: int32 [32, 32, 64], P('nodes'), may hold values from 0 to 255
- query_head: int32 [32], P('queries'), may hold values from 0 to 8191
- query_rel: int32 [32], P('queries'), may hold values from 0 to 534
- pos_tail: int32 [32], P('queries'), may hold values from 0 to 8191
- neg_ids: int32 [32, 4096], P('queries', 'nodes'), may hold values from 0 to 255
- rel_table: float32 [535, 32], replicated, may hold values from -1.8 to 1.8
- layer_weight: float32 [32, 32], replicated, may hold values from -1 to 1
- mlp_entity: float32 [32, 64], replicated, may hold values from -1 to 1
- mlp_query: float32 [32, 64], replicated, may hold values from -1 to 1
- score_weight: float32 [64], replicated, may hold values from -0.75 to 0.75
Outputs:
- new_state: float32 [8192, 1024], P('nodes', 'queries')
- loss: float32 [32], P('queries')
- grad_rel: float32 [535, 32], replicated
- grad_layer: float32 [32, 32], replicated
- grad_entity: float32 [32, 64], replicated
- grad_query: float32 [32, 64], replicated
- grad_score: float32 [64], replicated
The draws below stay inside these ranges and needn't reach their ends.
Inputs may be any that keep to these rules, and one draw needn't show every extreme that they name: `edge_count`: some partition holds exactly 4096 live edges.
All inputs are finite; a program needn't handle non-finite values.
Results may differ from the reference program's by a relative error of at most 0.0003.
Values sent between devices are 32-bit elements; how exact they have to be, the bound alone decides.
A program may use at most 64 MiB of HBM per device.

```python
import math
import jax
import jax.numpy as jnp
import numpy as np
from jax import lax

D = 32
NREL = 535
HID = 64
ENT_DEV = 256
NEG_DEV = 128
BND = 64
ENTITIES = 8192
QUERIES = 32
NEG = 4096
EDGE_DEV = 4096
HALO = 2048
N_NODES = 32


def draw_state_in(key, part):
    first_key, second_key = jax.random.split(key, 2)
    ramp = 0.5 + jnp.arange(ENTITIES, dtype=jnp.float32) / ENTITIES
    rough = jnp.exp(jax.random.uniform(second_key, (ENTITIES, 1), jnp.float32, 0.0, math.log(3.0)))
    values = jax.random.normal(first_key, (ENTITIES, QUERIES * D), jnp.float32)
    return (ramp[:, None] * rough * values).astype(jnp.float32)


def draw_edge_count(key, part):
    counts = jax.random.randint(key, (N_NODES,), EDGE_DEV // 4, EDGE_DEV + 1, jnp.int32)
    fullest = jax.random.randint(jax.random.fold_in(key, 7), (), 0, N_NODES, jnp.int32)
    return counts.at[fullest].set(EDGE_DEV)


def set_ends(drawn, rng, least, high):
    spot = [jax.random.randint(jax.random.fold_in(rng, axis), (), 0, length) for axis, length in enumerate(drawn.shape)]
    longest = drawn.shape.index(max(drawn.shape))
    beside = spot[:longest] + [(spot[longest] + 1) % drawn.shape[longest]] + spot[longest + 1:]
    return drawn.at[tuple(spot)].set(least).at[tuple(beside)].set(high)


def rank_bounds(amount, slope):
    weights = [(1 << 20) // math.isqrt(standing ** slope) + 1 for standing in range(1, amount + 1)]
    scale = 1 + sum(weights) // (1 << 30)
    return np.cumsum(np.array([max(1, weight // scale) for weight in weights]))


def ranked_ids(key, extent, count, slope):
    table = rank_bounds(count, slope)
    ticket = jax.random.randint(jax.random.fold_in(key, 1), extent, 0, int(table[count - 1]))
    standing = jnp.searchsorted(jnp.asarray(table, jnp.int32), ticket, side="right")
    return jax.random.permutation(jax.random.fold_in(key, 2), count)[standing].astype(jnp.int32)


def gaussian(key, extent, scale, limit, kind=jnp.bfloat16):
    values = jax.random.normal(key, extent, jnp.float32) * scale
    return jnp.minimum(jnp.maximum(values, -limit), limit).astype(kind)


def setup_inputs(seed: int = 0) -> dict:
    seeds = jax.random.split(jax.random.key(seed), 16)
    return {
        "state_in": draw_state_in(jax.random.fold_in(seeds[15], 71), 0),
        "edge_src": set_ends(jax.random.randint(seeds[1], (N_NODES * EDGE_DEV,), 0, ENT_DEV + HALO), jax.random.fold_in(seeds[1], 1), 0, (ENT_DEV + HALO) - 1).astype(jnp.int32),
        "edge_dst": set_ends(jax.random.randint(seeds[2], (N_NODES * EDGE_DEV,), 0, ENT_DEV), jax.random.fold_in(seeds[2], 1), 0, ENT_DEV - 1).astype(jnp.int32),
        "edge_rel": set_ends(ranked_ids(seeds[3], (N_NODES * EDGE_DEV,), NREL, 2), jax.random.fold_in(seeds[3], 3), 0, NREL - 1).astype(jnp.int32),
        "edge_count": draw_edge_count(jax.random.fold_in(seeds[15], 71), 0),
        "send_list": set_ends(jax.random.randint(seeds[5], (N_NODES, N_NODES, BND), 0, ENT_DEV), jax.random.fold_in(seeds[5], 1), 0, ENT_DEV - 1).astype(jnp.int32),
        "query_head": set_ends(jax.random.randint(seeds[6], (QUERIES,), 0, ENTITIES), jax.random.fold_in(seeds[6], 1), 0, ENTITIES - 1).astype(jnp.int32),
        "query_rel": set_ends(jax.random.randint(seeds[7], (QUERIES,), 0, NREL), jax.random.fold_in(seeds[7], 1), 0, NREL - 1).astype(jnp.int32),
        "pos_tail": set_ends(jax.random.randint(seeds[8], (QUERIES,), 0, ENTITIES), jax.random.fold_in(seeds[8], 1), 0, ENTITIES - 1).astype(jnp.int32),
        "neg_ids": set_ends(jax.random.randint(seeds[9], (QUERIES, NEG), 0, ENT_DEV), jax.random.fold_in(seeds[9], 1), 0, ENT_DEV - 1).astype(jnp.int32),
        "rel_table": gaussian(seeds[10], (NREL, D), 0.3, 1.8, jnp.float32),
        "layer_weight": gaussian(seeds[11], (D, D), D ** -0.5, 1.0, jnp.float32),
        "mlp_entity": gaussian(seeds[12], (D, HID), D ** -0.5, 1.0, jnp.float32),
        "mlp_query": gaussian(seeds[13], (D, HID), D ** -0.5, 1.0, jnp.float32),
        "score_weight": gaussian(seeds[14], (HID,), HID ** -0.5, 0.75, jnp.float32),
    }


adversarial = 0.5


def edge_block(part_index, edge_src, edge_dst, edge_rel, edge_count, send_list):
    start = part_index * EDGE_DEV
    src_slot = lax.dynamic_slice_in_dim(edge_src, start, EDGE_DEV)
    dst_slot = lax.dynamic_slice_in_dim(edge_dst, start, EDGE_DEV)
    rel_slot = lax.dynamic_slice_in_dim(edge_rel, start, EDGE_DEV)
    remote = jnp.maximum(src_slot - ENT_DEV, 0).astype(jnp.int32)
    provider = (remote // BND).astype(jnp.int32)
    position = (remote % BND).astype(jnp.int32)
    far_entity = send_list[provider, part_index, position]
    source = jnp.where(src_slot < ENT_DEV, part_index * ENT_DEV + src_slot, provider * ENT_DEV + far_entity).astype(jnp.int32)
    live_mask = (jnp.arange(EDGE_DEV) < edge_count[part_index]).astype(jnp.float32)
    return source, dst_slot, rel_slot, live_mask


def reference(state_in, edge_src, edge_dst, edge_rel, edge_count, send_list, query_head, query_rel, pos_tail, neg_ids, rel_table, layer_weight, mlp_entity, mlp_query, score_weight):
    high = lax.Precision.HIGHEST
    state_cube = state_in.reshape(ENTITIES, QUERIES, D)
    parts = jnp.arange(N_NODES, dtype=jnp.int32)

    def forward_part(part_index):
        source, dst_slot, rel_slot, live_mask = edge_block(part_index, edge_src, edge_dst, edge_rel, edge_count, send_list)
        rel_rows = rel_table[rel_slot] * live_mask[:, None]
        message = state_cube[source] * rel_rows[:, None, :]
        return jax.ops.segment_sum(message, dst_slot, num_segments=ENT_DEV)

    summed = lax.map(forward_part, parts).reshape(ENTITIES, QUERIES, D)
    query_vec = rel_table[query_rel]
    head_mask = (jnp.arange(ENTITIES)[:, None] == query_head[None, :]).astype(jnp.float32)
    summed = summed + head_mask[:, :, None] * query_vec[None, :, :]
    pre_act = jnp.einsum('eqd,df->eqf', summed, layer_weight, precision=high)
    new_cube = state_cube + jax.nn.relu(pre_act)

    query_ids = jnp.arange(QUERIES)[:, None]
    negative_entity = ((jnp.arange(NEG) // NEG_DEV) * ENT_DEV)[None, :].astype(jnp.int32) + neg_ids
    pick_rows = jnp.concatenate([negative_entity, pos_tail[:, None]], axis=1)
    picked = new_cube[pick_rows, query_ids]
    hidden_pre = jnp.einsum('qrd,dh->qrh', picked, mlp_entity, precision=high) + jnp.dot(query_vec, mlp_query, precision=high)[:, None, :]
    hidden_act = jax.nn.relu(hidden_pre)
    scores = jnp.einsum('qrh,h->qr', hidden_act, score_weight, precision=high)
    neg_scores = scores[:, :-1]
    pos_score = scores[:, -1]
    weights_exp = jnp.exp(adversarial * neg_scores)
    total = jnp.sum(weights_exp, axis=1)
    loss = jax.nn.softplus(-pos_score) + jnp.sum(weights_exp * jax.nn.softplus(neg_scores), axis=1) / total
    neg_coeff = weights_exp / total[:, None] * jax.nn.sigmoid(neg_scores) / QUERIES
    pos_coeff = (jax.nn.sigmoid(pos_score) - 1.0) / QUERIES
    coeffs = jnp.concatenate([neg_coeff, pos_coeff[:, None]], axis=1)

    grad_hidden = coeffs[:, :, None] * score_weight[None, None, :] * (hidden_pre > 0).astype(jnp.float32)
    grad_score = jnp.einsum('qr,qrh->h', coeffs, hidden_act, precision=high)
    grad_entity = jnp.einsum('qrd,qrh->dh', picked, grad_hidden, precision=high)
    hidden_total = jnp.sum(grad_hidden, axis=1)
    grad_query = jnp.dot(query_vec.T, hidden_total, precision=high)
    grad_picked = jnp.einsum('qrh,dh->qrd', grad_hidden, mlp_entity, precision=high)
    grad_qvec = jnp.dot(hidden_total, mlp_query.T, precision=high)
    grad_cube = jnp.zeros((ENTITIES, QUERIES, D), jnp.float32).at[pick_rows, query_ids].add(grad_picked)
    grad_pre = grad_cube * (pre_act > 0).astype(jnp.float32)
    grad_layer = jnp.einsum('eqd,eqf->df', summed, grad_pre, precision=high)
    grad_sum = jnp.einsum('eqf,df->eqd', grad_pre, layer_weight, precision=high)
    grad_qvec = grad_qvec + grad_sum[query_head, jnp.arange(QUERIES)]

    def backward_part(part_index):
        source, dst_slot, rel_slot, live_mask = edge_block(part_index, edge_src, edge_dst, edge_rel, edge_count, send_list)
        upstream = grad_sum[part_index * ENT_DEV + dst_slot]
        edge_terms = jnp.einsum('eqd,eqd->ed', upstream, state_cube[source], precision=high) * live_mask[:, None]
        return jax.ops.segment_sum(edge_terms, rel_slot, num_segments=NREL)

    grad_rel = jnp.sum(lax.map(backward_part, parts), axis=0)
    grad_rel = grad_rel + jax.ops.segment_sum(grad_qvec, query_rel, num_segments=NREL)
    new_state = new_cube.reshape(ENTITIES, QUERIES * D)
    return (new_state, loss, grad_rel, grad_layer, grad_entity, grad_query, grad_score)
```

```python
import functools

import jax
import jax.numpy as jnp
from jax import lax
from jax.experimental import pallas as pl
from jax.experimental.pallas import tpu as pltpu
from jax.sharding import PartitionSpec as P

adversarial = 0.5
MESH = pl.DeviceIdType.MESH
HIGH = lax.Precision.HIGHEST
F32 = jnp.float32
BF16 = jnp.bfloat16
NT = (((1,), (1,)), ((), ()))
NN = (((1,), (0,)), ((), ()))
TILES = 24
RELP = 640
BLK = 256


def mm(a, b, dims=NN, precision=None):
    return lax.dot_general(a, b, dims, precision=precision, preferred_element_type=F32)


def split(x, terms):
    parts = []
    for i in range(terms):
        part = x.astype(BF16)
        parts.append(part)
        if i + 1 < terms:
            x = x - part.astype(F32)
    return jnp.concatenate(parts, axis=0)


def join(y, terms):
    rows = y.shape[0] // terms
    out = y[:rows]
    for i in range(1, terms):
        out = out + y[i * rows : (i + 1) * rows]
    return out


def onehot(row, depth, base=0):
    ids = lax.broadcasted_iota(jnp.int32, (depth, row.shape[1]), 0)
    return jnp.where(ids == row - base, 1.0, 0.0).astype(BF16)


def lanes_of(x, queries, rows):
    return jnp.concatenate([x[q * rows : (q + 1) * rows] for q in range(queries)], axis=1)


def softplus(x):
    return jnp.maximum(x, 0.0) + jnp.log1p(jnp.exp(-jnp.abs(x)))


def sigmoid(x):
    return 1.0 / (1.0 + jnp.exp(-x))


def kernel(
    cfg,
    state, esrc, edst, erel, slist, neg, rel, wl, me_w, mq_w, sw, ecount, qhead, qrel, ptail,
    new_out, loss_out, grel_out, glayer_out, gent_out, gquery_out, gscore_out,
    st3, slrow, relpad, rt3, sbuf, recv, ort, odt, relg, acc, msg3, et2, onr,
    tsend, trecv, gmat, rsrc, rsbuf, zbuf, agbuf,
    s_send, s_recv, t_send, t_recv, r_send, r_recv, z_send, z_recv, a_send, a_recv,
):
    nodes, zs, nx, ny, queries_total = cfg
    me = lax.axis_index("nodes")
    mz = lax.axis_index("queries")
    chip = me // 2
    core = me % 2
    cx = chip % nx
    cy = chip // nx
    chips = nx * ny
    dd = wl.shape[0]
    hid = me_w.shape[1]
    ent = state.shape[0]
    nq = state.shape[1] // dd
    edges = esrc.shape[0] * 128
    blocks = edges // BLK
    negs = neg.shape[1]
    nrel = rel.shape[0]
    lane128 = lax.broadcasted_iota(jnp.int32, (1, 128), 1)
    low = lane128 < 64

    def node_of(t):
        return (t, mz)

    barrier = pltpu.get_barrier_semaphore()

    @pl.loop(1, nodes)
    def _(k):
        pl.semaphore_signal(barrier, inc=1, device_id=node_of((me + k) % nodes), device_id_type=MESH)

    @pl.loop(1, zs)
    def _(k):
        pl.semaphore_signal(barrier, inc=1, device_id=(me, (mz + k) % zs), device_id_type=MESH)

    stt = jnp.concatenate([state[i * 128 : (i + 1) * 128, :].T for i in range(ent // 128)], axis=1)
    st3[...] = split(stt, 3)
    slrow[:, 0:64] = slist[...]
    slrow[:, 64:128] = slist[...]

    pl.semaphore_wait(barrier, nodes - 1 + zs - 1)

    def chip_at(s, sign):
        tx = (cx + sign * (s % nx) + nx) % nx
        ty = (cy + sign * (s // nx) + ny) % ny
        return ty * nx + tx

    @pl.loop(0, chips)
    def _(s):
        tc = chip_at(s, 1)
        row = jnp.where(low, slrow[pl.ds(2 * tc, 1), :], slrow[pl.ds(2 * tc + 1, 1), :])
        got = join(mm(st3[...], onehot(row, ent)), 3)
        top, bot = got[:64], got[64:]
        c0 = jnp.where(low, top, pltpu.roll(bot, 64, 1))
        c1 = jnp.where(low, pltpu.roll(top, 64, 1), bot)
        sbuf[2 * s] = c0
        sbuf[2 * s + 1] = c1
        for c in range(2):
            @pl.when((s > 0) | (core != c))
            def _():
                pltpu.make_async_remote_copy(
                    src_ref=sbuf.at[2 * s + c],
                    dst_ref=recv.at[2 * s + core],
                    send_sem=s_send.at[2 * s + c],
                    recv_sem=s_recv.at[2 * s + core],
                    device_id=node_of(2 * tc + c),
                    device_id_type=MESH,
                ).start()

    recv[core] = sbuf[core]

    relpad[...] = jnp.zeros_like(relpad)
    relpad[0:nrel, 0:dd] = rel[...]
    relt = jnp.concatenate([relpad[i * 128 : (i + 1) * 128, :].T[:dd] for i in range(RELP // 128)], axis=1)
    rt3[...] = split(relt, 3)

    def edge_row(ref, j):
        return jnp.concatenate([ref[pl.ds(2 * j, 1), :], ref[pl.ds(2 * j + 1, 1), :]], axis=1)

    def cols(j):
        return pl.ds(pl.multiple_of(j * BLK, BLK), BLK)

    lane256 = lax.broadcasted_iota(jnp.int32, (1, BLK), 1)

    @pl.loop(0, blocks)
    def _(j):
        hot = onehot(edge_row(erel, j), RELP)
        ort[:, cols(j)] = hot
        relg[:, cols(j)] = join(mm(rt3[...], hot), 3)
        dst = jnp.where(lane256 + j * BLK < ecount[0], edge_row(edst, j), -1)
        odt[:, cols(j)] = onehot(dst, ent)
        acc[:, cols(j)] = join(mm(st3[...], onehot(edge_row(esrc, j), ent)), 3)

    @pl.loop(0, chips // 2)
    def _(t):
        for k in range(4):
            slot = 4 * t + k

            @pl.when((t > 0) | (k != core))
            def _():
                pltpu.make_async_copy(recv.at[slot], recv.at[slot], s_recv.at[slot]).wait()

        def pair(i):
            a, b = recv[4 * t + 2 * i], recv[4 * t + 2 * i + 1]
            top = jnp.where(low, a, pltpu.roll(b, 64, 1))
            bot = jnp.where(low, pltpu.roll(a, 64, 1), b)
            return jnp.concatenate([top, bot], axis=0)

        part = split(jnp.concatenate([pair(0), pair(1)], axis=1), 3)
        base0 = ent + 128 * chip_at(2 * t, -1)
        base1 = ent + 128 * chip_at(2 * t + 1, -1)

        @pl.loop(0, blocks)
        def _(j):
            row = edge_row(esrc, j)
            hot = jnp.concatenate([onehot(row, 128, base0), onehot(row, 128, base1)], axis=0)
            acc[:, cols(j)] += join(mm(part, hot), 3)

    @pl.loop(0, blocks)
    def _(j):
        r = relg[:, cols(j)]
        msg3[:, cols(j)] = split(acc[:, cols(j)] * jnp.concatenate([r] * nq, axis=0), 3)

    summed = join(mm(msg3[...], odt[...], NT), 3)

    def scalar_lanes(ref):
        out = jnp.full((1, 128), -1, jnp.int32)
        for q in range(nq):
            out = jnp.where(lane128 == q, ref[q], out)
        return out

    relhot = onehot(scalar_lanes(qrel), RELP)
    qvt = join(mm(rt3[...], relhot), 3)
    lane_ent = lax.broadcasted_iota(jnp.int32, (1, ent), 1)

    def local_of(g):
        return jnp.where(g // ent == me, g % ent, -1)

    heads = [jnp.where(lane_ent == local_of(qhead[q]), 1.0, 0.0) for q in range(nq)]
    s_all = lanes_of(summed, nq, dd) + jnp.concatenate(
        [qvt[:, q : q + 1] * heads[q] for q in range(nq)], axis=1
    )
    stt = jnp.concatenate([state[i * 128 : (i + 1) * 128, :].T for i in range(ent // 128)], axis=1)
    pre = mm(wl[...].T, s_all, precision=HIGH)
    new_all = lanes_of(stt, nq, dd) + jnp.maximum(pre, 0.0)
    new_t = jnp.concatenate([new_all[:, q * ent : (q + 1) * ent] for q in range(nq)], axis=0)
    for i in range(ent // 128):
        new_out[i * 128 : (i + 1) * 128, :] = new_t[:, i * 128 : (i + 1) * 128].T

    rows = 2 * negs
    lane_row = lax.broadcasted_iota(jnp.int32, (1, rows), 1)
    picks = []
    pos_mask = []
    for q in range(nq):
        pos = local_of(ptail[q])
        pos_mask.append((lane_row == negs) & (pos >= 0))
        wide = jnp.concatenate([neg[q : q + 1, :], jnp.full((1, negs), 0, jnp.int32) + pos], axis=1)
        hot = onehot(jnp.where(lane_row <= negs, wide, -1), ent)
        onr[q] = hot
        picks.append(join(mm(split(new_t[q * dd : (q + 1) * dd], 3), hot), 3))
    picked = jnp.concatenate(picks, axis=1)
    is_neg = jnp.concatenate([lane_row < negs] * nq, axis=1)
    is_pos = jnp.concatenate(pos_mask, axis=1)
    qh = mm(mq_w[...].T, qvt, precision=HIGH)
    pre_h = mm(me_w[...].T, picked, precision=HIGH) + jnp.concatenate(
        [jnp.broadcast_to(qh[:, q : q + 1], (hid, rows)) for q in range(nq)], axis=1
    )
    act = jnp.maximum(pre_h, 0.0)
    eye = lax.broadcasted_iota(jnp.int32, (hid, hid), 0) == lax.broadcasted_iota(jnp.int32, (hid, hid), 1)
    swc = jnp.sum(jnp.where(eye, sw[...], 0.0), axis=1, keepdims=True)
    score = jnp.sum(act * swc, axis=0, keepdims=True)
    weight = jnp.where(is_neg, jnp.exp(adversarial * score), 0.0)
    weighted = jnp.where(is_neg, weight * softplus(score), 0.0)
    positive = jnp.where(is_pos, softplus(-score), 0.0)
    line = jnp.zeros((1, 128), F32)
    for q in range(nq):
        lanes = slice(q * rows, (q + 1) * rows)
        for k, value in enumerate((weight, weighted, positive)):
            total = jnp.sum(value[:, lanes], axis=1, keepdims=True)
            line = jnp.where(lane128 == k * nq + q, total, line)
    tsend[...] = line
    trecv[me] = line

    @pl.loop(1, nodes)
    def _(k):
        pltpu.make_async_remote_copy(
            src_ref=tsend,
            dst_ref=trecv.at[me],
            send_sem=t_send,
            recv_sem=t_recv,
            device_id=node_of((me + k) % nodes),
            device_id_type=MESH,
        ).start()

    pltpu.make_async_copy(trecv.at[pl.ds(0, nodes - 1)], trecv.at[pl.ds(0, nodes - 1)], t_recv).wait()
    totals = jnp.sum(trecv[...], axis=0)
    loss_out[...] = totals[:, 2 * nq : 3 * nq] + totals[:, nq : 2 * nq] / totals[:, :nq]

    total_row = jnp.concatenate(
        [jnp.broadcast_to(totals[:, q : q + 1], (1, rows)) for q in range(nq)], axis=1
    )
    sig = sigmoid(score)
    coef = jnp.where(is_neg, weight / total_row * sig, jnp.where(is_pos, sig - 1.0, 0.0)) / queries_total
    gh = coef * swc * jnp.where(pre_h > 0, 1.0, 0.0)
    gscore = mm(jnp.broadcast_to(coef, (8, nq * rows)), act, NT, HIGH)[0:1]
    ht = jnp.zeros((hid, 128), F32)
    for q in range(nq):
        col = jnp.sum(gh[:, q * rows : (q + 1) * rows], axis=1, keepdims=True)
        ht = jnp.where(lane128 == q, col, ht)
    gqt = mm(mq_w[...], ht, precision=HIGH)
    gquery = mm(qvt, ht, NT, HIGH)
    gent = mm(picked, gh, NT, HIGH)
    gp = mm(me_w[...], gh, precision=HIGH)
    gc = jnp.concatenate(
        [join(mm(split(gp[:, q * rows : (q + 1) * rows], 3), onr[q], NT), 3) for q in range(nq)], axis=1
    )
    gpre = jnp.where(pre > 0, gc, 0.0)
    glayer = mm(s_all, gpre, NT, HIGH)
    gsum = mm(wl[...], gpre, precision=HIGH)
    for q in range(nq):
        col = jnp.sum(gsum[:, q * ent : (q + 1) * ent] * heads[q], axis=1, keepdims=True)
        gqt = gqt + jnp.where(lane128 == q, col, 0.0)
    gs2 = split(jnp.concatenate([gsum[:, q * ent : (q + 1) * ent] for q in range(nq)], axis=0), 2)

    @pl.loop(0, blocks)
    def _(j):
        up = join(mm(gs2, odt[:, cols(j)]), 2) * acc[:, cols(j)]
        et2[:, cols(j)] = split(join(up, nq), 2)

    grel = join(mm(et2[...], ort[...], NT), 2) + join(mm(split(gqt, 3), relhot, NT), 3)

    gmat[...] = jnp.zeros_like(gmat)
    gmat[:, 0:RELP] = grel
    gmat[:, 544 : 544 + dd] = glayer
    gmat[:, 576 : 576 + hid] = gent
    gmat[:, 640 : 640 + hid] = gquery
    gmat[0:1, 704 : 704 + hid] = gscore
    for c in range(6):
        for r in range(4):
            rsrc[c * 4 + r] = gmat[r * 8 : r * 8 + 8, c * 128 : (c + 1) * 128]

    own = me < TILES

    @pl.loop(1, nodes)
    def _(k):
        to = (me + k) % nodes

        @pl.when(to < TILES)
        def _():
            pltpu.make_async_remote_copy(
                src_ref=rsrc.at[to],
                dst_ref=rsbuf.at[me],
                send_sem=r_send,
                recv_sem=r_recv,
                device_id=node_of(to),
                device_id_type=MESH,
            ).start()

    @pl.when(own)
    def _():
        rsbuf[me] = rsrc[me]
        pltpu.make_async_copy(rsbuf.at[pl.ds(0, nodes - 1)], rsbuf.at[pl.ds(0, nodes - 1)], r_recv).wait()
        zbuf[mz] = jnp.sum(rsbuf[...], axis=0)

        @pl.loop(1, zs)
        def _(k):
            pltpu.make_async_remote_copy(
                src_ref=zbuf.at[mz],
                dst_ref=zbuf.at[mz],
                send_sem=z_send,
                recv_sem=z_recv,
                device_id=(me, (mz + k) % zs),
                device_id_type=MESH,
            ).start()

        if zs > 1:
            pltpu.make_async_copy(zbuf.at[pl.ds(0, zs - 1)], zbuf.at[pl.ds(0, zs - 1)], z_recv).wait()
        agbuf[me] = jnp.sum(zbuf[...], axis=0)

        @pl.loop(1, nodes)
        def _(k):
            pltpu.make_async_remote_copy(
                src_ref=agbuf.at[me],
                dst_ref=agbuf.at[me],
                send_sem=a_send,
                recv_sem=a_recv,
                device_id=node_of((me + k) % nodes),
                device_id_type=MESH,
            ).start()

        pltpu.make_async_copy(agbuf.at[pl.ds(0, TILES - 1)], agbuf.at[pl.ds(0, TILES - 1)], a_recv).wait()

    @pl.when(jnp.logical_not(own))
    def _():
        pltpu.make_async_copy(agbuf, agbuf, a_recv).wait()

    for c in range(6):
        for r in range(4):
            gmat[r * 8 : r * 8 + 8, c * 128 : (c + 1) * 128] = agbuf[c * 4 + r]
    for i in range(RELP // 128):
        first, last = i * 128, min(i * 128 + 128, nrel)
        wide = jnp.concatenate([gmat[:, first : first + 128]] * 4, axis=0).T
        grel_out[first:last, :] = wide[: last - first, :dd]
    glayer_out[...] = gmat[:, 544 : 544 + dd]
    gent_out[...] = gmat[:, 576 : 576 + hid]
    gquery_out[...] = gmat[:, 640 : 640 + hid]
    gscore_out[...] = gmat[0:1, 704 : 704 + hid]

    @pl.loop(0, 2 * chips)
    def _(i):
        @pl.when(i != core)
        def _():
            pltpu.make_async_copy(sbuf.at[i], sbuf.at[i], s_send.at[i]).wait()

    pltpu.make_async_copy(trecv.at[pl.ds(0, nodes - 1)], trecv.at[pl.ds(0, nodes - 1)], t_send).wait()

    @pl.when(own)
    def _():
        pltpu.make_async_copy(agbuf.at[pl.ds(0, TILES - 1)], agbuf.at[pl.ds(0, TILES - 1)], r_send).wait()
        if zs > 1:
            pltpu.make_async_copy(zbuf.at[pl.ds(0, zs - 1)], zbuf.at[pl.ds(0, zs - 1)], z_send).wait()
        pltpu.make_async_copy(rsbuf.at[pl.ds(0, nodes - 1)], rsbuf.at[pl.ds(0, nodes - 1)], a_send).wait()

    @pl.when(jnp.logical_not(own))
    def _():
        pltpu.make_async_copy(agbuf, agbuf, r_send).wait()


def body(
    sizes,
    state_in, edge_src, edge_dst, edge_rel, edge_count, send_list, query_head, query_rel, pos_tail,
    neg_ids, rel_table, layer_weight, mlp_entity, mlp_query, score_weight,
):
    nodes, zs, nx, ny = sizes
    ent, width = state_in.shape
    dd = rel_table.shape[1]
    hid = mlp_entity.shape[1]
    nq = width // dd
    nrel = rel_table.shape[0]
    edges = edge_src.shape[0]
    negs = neg_ids.shape[1]
    sds = jax.ShapeDtypeStruct
    vmem = pl.BlockSpec(memory_space=pltpu.VMEM)
    smem = pl.BlockSpec(memory_space=pltpu.SMEM)
    dma = pltpu.SemaphoreType.DMA
    scratch = [
        pltpu.VMEM((3 * width, ent), BF16),
        pltpu.VMEM((nodes, 128), jnp.int32),
        pltpu.VMEM((RELP, 128), F32),
        pltpu.VMEM((3 * dd, RELP), BF16),
        pltpu.VMEM((nodes, 64, 128), F32),
        pltpu.VMEM((nodes, 64, 128), F32),
        pltpu.VMEM((RELP, edges), BF16),
        pltpu.VMEM((ent, edges), BF16),
        pltpu.VMEM((dd, edges), F32),
        pltpu.VMEM((width, edges), F32),
        pltpu.VMEM((3 * width, edges), BF16),
        pltpu.VMEM((2 * dd, edges), BF16),
        pltpu.VMEM((nq, ent, 2 * negs), BF16),
        pltpu.VMEM((1, 128), F32),
        pltpu.VMEM((nodes, 1, 128), F32),
        pltpu.VMEM((dd, 768), F32),
        pltpu.VMEM((TILES, 8, 128), F32),
        pltpu.VMEM((nodes, 8, 128), F32),
        pltpu.VMEM((zs, 8, 128), F32),
        pltpu.VMEM((TILES, 8, 128), F32),
        dma((nodes,)), dma((nodes,)), dma, dma, dma, dma, dma, dma, dma, dma,
    ]
    out = pl.pallas_call(
        functools.partial(kernel, (nodes, zs, nx, ny, nq * zs)),
        out_shape=(
            sds((ent, width), F32),
            sds((1, nq), F32),
            sds((nrel, dd), F32),
            sds((dd, dd), F32),
            sds((dd, hid), F32),
            sds((dd, hid), F32),
            sds((1, hid), F32),
        ),
        in_specs=[vmem] * 11 + [smem] * 4,
        out_specs=[vmem] * 7,
        scratch_shapes=scratch,
        compiler_params=pltpu.CompilerParams(
            collective_id=0, has_side_effects=True, vmem_limit_bytes=48 << 20
        ),
        name="layer",
    )(
        state_in,
        edge_src.reshape(edges // 128, 128),
        edge_dst.reshape(edges // 128, 128),
        edge_rel.reshape(edges // 128, 128),
        send_list.reshape(nodes, 64),
        neg_ids,
        rel_table,
        layer_weight,
        mlp_entity,
        mlp_query,
        score_weight.reshape(1, hid),
        edge_count,
        query_head,
        query_rel,
        pos_tail,
    )
    new_state, loss, grel, glayer, gent, gquery, gscore = out
    return new_state, loss.reshape(nq), grel, glayer, gent, gquery, gscore.reshape(hid)


def solution(mesh):
    nodes, zs = mesh.shape["nodes"], mesh.shape["queries"]
    nx = 4
    ny = nodes // (2 * nx)
    in_specs = (
        P("nodes", "queries"),
        P("nodes"),
        P("nodes"),
        P("nodes"),
        P("nodes"),
        P("nodes", None, None),
        P("queries"),
        P("queries"),
        P("queries"),
        P("queries", "nodes"),
        P(),
        P(),
        P(),
        P(),
        P(),
    )
    out_specs = (P("nodes", "queries"), P("queries"), P(), P(), P(), P(), P())
    return jax.shard_map(
        functools.partial(body, (nodes, zs, nx, ny)),
        mesh=mesh, in_specs=in_specs, out_specs=out_specs, check_vma=False,
    )
```

```python
import functools

import jax
import jax.numpy as jnp
from jax import lax
from jax.experimental import pallas as pl
from jax.experimental.pallas import tpu as pltpu
from jax.sharding import PartitionSpec as P

adversarial = 0.5
MESH = pl.DeviceIdType.MESH
HIGH = lax.Precision.HIGHEST
F32 = jnp.float32
BF16 = jnp.bfloat16
NT = (((1,), (1,)), ((), ()))
NN = (((1,), (0,)), ((), ()))
TILES = 24
BLK = 256
WIDE = 512


def mm(a, b, dims=NN, precision=None):
    return lax.dot_general(a, b, dims, precision=precision, preferred_element_type=F32)


def parts_of(x, terms):
    parts = []
    for i in range(terms):
        part = x.astype(BF16)
        parts.append(part)
        if i + 1 < terms:
            x = x - part.astype(F32)
    return parts


def split(x, terms, axis=0):
    return jnp.concatenate(parts_of(x, terms), axis=axis)


def join(y, terms):
    rows = y.shape[0] // terms
    out = y[:rows]
    for i in range(1, terms):
        out = out + y[i * rows : (i + 1) * rows]
    return out


def onehot(row, depth):
    ids = lax.broadcasted_iota(jnp.int32, (depth, row.shape[1]), 0)
    return jnp.where(ids == row, 1.0, 0.0).astype(BF16)


def lanes_of(x, queries, rows):
    return jnp.concatenate([x[q * rows : (q + 1) * rows] for q in range(queries)], axis=1)


def rows_of(x, queries, width):
    return jnp.concatenate([x[:, q * width : (q + 1) * width] for q in range(queries)], axis=0)


def transposed(x):
    r, c = x.shape
    return jnp.concatenate(
        [
            jnp.concatenate([x[i : i + 128, j : j + 128].T for i in range(0, r, 128)], axis=1)
            for j in range(0, c, 128)
        ],
        axis=0,
    )


def softplus(x):
    return jnp.maximum(x, 0.0) + jnp.log1p(jnp.exp(-jnp.abs(x)))


def sigmoid(x):
    return 1.0 / (1.0 + jnp.exp(-x))


def far_first(nx, ny):
    def away(d, n):
        return min(d, n - d)

    steps = [(dx, dy) for dy in range(ny) for dx in range(nx) if (dx, dy) != (0, 0)]
    return sorted(steps, key=lambda s: (-away(s[0], nx) - away(s[1], ny), s))


def kernel(
    cfg,
    h_state, h_esrc, h_edst, h_erel, h_slist, h_neg, h_rel, h_wl, h_me, h_mq, h_sw,
    h_count, h_head, h_qrel, h_tail,
    new_out, loss_out, ag,
    st_v, tab, sbuf, edst, erel, neg, relraw, wl, me_w, mq_w, sw,
    esrc, slist, ecount, qhead, qrel, ptail,
    relpad, rt9, stt_ref, relrow, ort, odt, srcr, srct, msg3, acc, et6,
    tsend, trecv, gmat, rsrc, rsbuf, zbuf,
    i_sem, s_send, s_recv, t_send, t_recv, r_send, r_recv, z_send, z_recv, a_send, a_recv,
):
    nodes, zs, nx, ny, queries_total = cfg
    me = lax.axis_index("nodes")
    mz = lax.axis_index("queries")
    chip = me // 2
    core = me % 2
    cx = chip % nx
    cy = chip // nx
    dd, hid = me_w.shape
    ent = h_state.shape[0]
    nq = h_state.shape[1] // dd
    edges = h_esrc.shape[0]
    bnd = h_slist.shape[1]
    blocks = edges // BLK
    nrel = relraw.shape[1]
    lane128 = lax.broadcasted_iota(jnp.int32, (1, 128), 1)

    def node_of(t):
        return (t, mz)

    loads = [
        pltpu.make_async_copy(src, dst, i_sem.at[i])
        for i, (src, dst) in enumerate(
            (
                (h_slist, slist), (h_state, st_v), (h_state, tab.at[pl.ds(0, ent)]), (h_rel, relraw), (h_erel, erel),
                (h_edst, edst), (h_esrc, esrc), (h_count, ecount), (h_qrel, qrel), (h_head, qhead),
                (h_tail, ptail), (h_neg, neg), (h_wl, wl), (h_me, me_w), (h_mq, mq_w), (h_sw, sw),
            )
        )
    ]
    for load in loads:
        load.start()
    barrier = pltpu.get_barrier_semaphore()

    @pl.loop(1, nodes)
    def _(k):
        pl.semaphore_signal(barrier, inc=1, device_id=node_of((me + k) % nodes), device_id_type=MESH)

    @pl.loop(1, zs)
    def _(k):
        pl.semaphore_signal(barrier, inc=1, device_id=(me, (mz + k) % zs), device_id_type=MESH)

    loads[0].wait()
    loads[1].wait()

    @pl.loop(0, nodes)
    def _(b):
        for k in range(bnd):
            sbuf[pl.ds(b * bnd + k, 1), :] = st_v[pl.ds(slist[b, k], 1), :]

    pl.semaphore_wait(barrier, nodes - 1 + zs - 1)

    def chunk(first, n=1):
        return pl.ds(pl.multiple_of(first * bnd, bnd), n * bnd)

    def send_rows(to):
        pltpu.make_async_remote_copy(
            src_ref=sbuf.at[chunk(to)],
            dst_ref=tab.at[pl.ds(pl.multiple_of(ent + me * bnd, bnd), bnd)],
            send_sem=s_send,
            recv_sem=s_recv,
            device_id=node_of(to),
            device_id_type=MESH,
        ).start()

    for dx, dy in far_first(nx, ny):
        there = 2 * (((cy + dy) % ny) * nx + (cx + dx) % nx)
        send_rows(there + core)
        send_rows(there + 1 - core)
    send_rows(2 * chip + 1 - core)
    tab[pl.ds(pl.multiple_of(ent + me * bnd, bnd), bnd), :] = sbuf[chunk(me), :]

    for load in loads[2:]:
        load.wait()
    stt_ref[...] = transposed(st_v[...])
    relpad[...] = jnp.zeros_like(relpad)
    relpad[:, 0:nrel] = relraw[...]
    rt9[...] = jnp.concatenate([split(relpad[:, h * 256 : (h + 1) * 256], 3) for h in range(3)], axis=0)

    def edge_row(ref, j):
        return jnp.concatenate([ref[pl.ds(2 * j, 1), :], ref[pl.ds(2 * j + 1, 1), :]], axis=1)

    def at_block(j, size=BLK):
        return pl.ds(pl.multiple_of(j * size, size), size)

    def relation(hot, high):
        got = mm(rt9[...], hot)
        out = jnp.zeros((dd, hot.shape[1]), F32)
        for h in range(3):
            out = jnp.where(high == h, join(got[h * 3 * dd : (h + 1) * 3 * dd], 3), out)
        return out

    lane256 = lax.broadcasted_iota(jnp.int32, (1, BLK), 1)

    @pl.loop(0, blocks)
    def _(j):
        row = edge_row(erel, j)
        hot = onehot(row & 255, 256)
        ort[:, at_block(j)] = hot
        relrow[at_block(j), :] = transposed(jnp.concatenate([relation(hot, row >> 8)] * nq, axis=0))
        dst = jnp.where(lane256 + j * BLK < ecount[0], edge_row(edst, j), -1)
        odt[:, at_block(j)] = onehot(dst, ent)

    qr = jnp.full((1, 128), -1, jnp.int32)
    for q in range(nq):
        qr = jnp.where(lane128 == q, qrel[q], qr)
    q_hot = onehot(qr & 255, 256)
    q_high = qr >> 8
    qvt = relation(q_hot, q_high)
    lane_ent = lax.broadcasted_iota(jnp.int32, (1, ent), 1)

    def local_of(g):
        return jnp.where(g // ent == me, g % ent, -1)

    heads = [jnp.where(lane_ent == local_of(qhead[q]), 1.0, 0.0) for q in range(nq)]
    tails = [jnp.where(lane_ent == local_of(ptail[q]), 1.0, 0.0) for q in range(nq)]
    head_term = jnp.concatenate([qvt[:, q : q + 1] * heads[q] for q in range(nq)], axis=1)
    qh = mm(mq_w[...].T, qvt, precision=HIGH)
    qh_wide = jnp.concatenate(
        [jnp.broadcast_to(qh[:, q : q + 1], (hid, 128)) for q in range(nq)] + [qh], axis=1
    )
    eye = lax.broadcasted_iota(jnp.int32, (hid, hid), 0) == lax.broadcasted_iota(jnp.int32, (hid, hid), 1)
    swc = jnp.sum(jnp.where(eye, sw[...], 0.0), axis=1, keepdims=True)
    acc[...] = jnp.zeros_like(acc)

    pltpu.make_async_copy(sbuf.at[chunk(0, nodes - 1)], sbuf.at[chunk(0, nodes - 1)], s_recv).wait()

    def gather(j):
        for u in range(BLK):
            srcr[pl.ds(j * BLK + u, 1), :] = tab[pl.ds(esrc[j * BLK + u], 1), :]
        msg3[at_block(j), :] = split(srcr[at_block(j), :] * relrow[at_block(j), :], 3, axis=1)

    def scatter(j):
        acc[...] += mm(odt[:, at_block(j)], msg3[at_block(j), :])

    gather(0)

    @pl.loop(1, blocks)
    def _(j):
        scatter(j - 1)
        gather(j)

    scatter(blocks - 1)
    width = nq * dd
    summed = acc[:, 0:width] + acc[:, width : 2 * width] + acc[:, 2 * width : 3 * width]
    s_all = lanes_of(transposed(summed), nq, dd) + head_term
    pre = mm(wl[...].T, s_all, precision=HIGH)
    new_all = lanes_of(stt_ref[...], nq, dd) + jnp.maximum(pre, 0.0)

    picks = []
    hots = []
    pos_pick = jnp.zeros((dd, 128), F32)
    is_pos = lane128 < 0
    for q in range(nq):
        mine = new_all[:, q * ent : (q + 1) * ent]
        ids = neg[q : q + 1, :]
        low = jnp.broadcast_to(ids & 127, (dd, 128))
        out = jnp.zeros((dd, 128), F32)
        for b in range(ent // 128):
            got = jnp.take_along_axis(
                mine[:, b * 128 : (b + 1) * 128], low, axis=1, mode="promise_in_bounds"
            )
            out = jnp.where((ids >> 7) == b, got, out)
        picks.append(out)
        hots.append(onehot(ids, ent))
        pos_pick = jnp.where(lane128 == q, jnp.sum(mine * tails[q], axis=1, keepdims=True), pos_pick)
        is_pos = is_pos | ((lane128 == q) & (ptail[q] // ent == me))
    picked = jnp.concatenate(picks + [pos_pick], axis=1)
    pre_h = mm(me_w[...].T, picked, precision=HIGH) + qh_wide
    act = jnp.maximum(pre_h, 0.0)
    score = jnp.sum(act * swc, axis=0, keepdims=True)
    nneg = nq * 128
    s_neg = rows_of(score[:, :nneg], nq, 128)
    s_pos = score[:, nneg:]
    weight = jnp.exp(adversarial * s_neg)
    part_total = jnp.sum(weight, axis=1, keepdims=True)
    part_weighted = jnp.sum(weight * softplus(s_neg), axis=1, keepdims=True)
    sub = lax.broadcasted_iota(jnp.int32, (nq, 128), 0)
    lanes = lax.broadcasted_iota(jnp.int32, (nq, 128), 1)

    def row_of(col, first):
        return jnp.sum(jnp.where(lanes == sub + first, col, 0.0), axis=0, keepdims=True)

    part_row = row_of(part_total, 0)
    pos_terms = jnp.where(is_pos, softplus(-s_pos), 0.0)
    line = part_row + row_of(part_weighted, nq) + pltpu.roll(pos_terms, 2 * nq, 1)
    tsend[...] = line
    trecv[me] = line

    @pl.loop(1, nodes)
    def _(k):
        pltpu.make_async_remote_copy(
            src_ref=tsend,
            dst_ref=trecv.at[me],
            send_sem=t_send,
            recv_sem=t_recv,
            device_id=node_of((me + k) % nodes),
            device_id_type=MESH,
        ).start()

    safe = jnp.where(part_total > 0, part_total, 1.0)
    c_neg = weight / safe * sigmoid(s_neg) / queries_total
    c_pos = jnp.where(is_pos, sigmoid(s_pos) - 1.0, 0.0) / queries_total
    coef = jnp.concatenate([c_neg[q : q + 1] for q in range(nq)] + [c_pos], axis=1)
    gh = coef * swc * jnp.where(pre_h > 0, 1.0, 0.0)
    gp = mm(me_w[...], gh, precision=HIGH)
    gc_neg = jnp.concatenate(
        [join(mm(split(gp[:, q * 128 : (q + 1) * 128], 3), hots[q], NT), 3) for q in range(nq)], axis=1
    )
    gc_pos = jnp.concatenate([gp[:, nneg + q : nneg + q + 1] * tails[q] for q in range(nq)], axis=1)
    gpre = jnp.concatenate([jnp.where(pre > 0, gc_neg, 0.0), jnp.where(pre > 0, gc_pos, 0.0)], axis=1)
    gsum = mm(wl[...], gpre, precision=HIGH)
    half = nq * ent
    gs_neg = rows_of(gsum[:, :half], nq, ent)
    gs_pos = rows_of(gsum[:, half:], nq, ent)

    ht_neg = jnp.zeros((hid, 128), F32)
    hd_neg = jnp.zeros((dd, 128), F32)
    hd_pos = jnp.zeros((dd, 128), F32)
    scores8 = jnp.broadcast_to(coef, (8, nneg + 128))
    ent_q, lay_q, sco_q = [], [], []
    lay_pos = jnp.zeros((dd, dd), F32)
    for q in range(nq):
        tile = slice(q * 128, (q + 1) * 128)
        cols = slice(q * ent, (q + 1) * ent)
        here = lane128 == q
        ht_neg = jnp.where(here, jnp.sum(gh[:, tile], axis=1, keepdims=True), ht_neg)
        hd_neg = jnp.where(here, jnp.sum(gsum[:, cols] * heads[q], axis=1, keepdims=True), hd_neg)
        g_p = gsum[:, half + q * ent : half + (q + 1) * ent]
        hd_pos = jnp.where(here, jnp.sum(g_p * heads[q], axis=1, keepdims=True), hd_pos)
        ent_q.append(mm(picked[:, tile], gh[:, tile], NT, HIGH))
        sco_q.append(mm(scores8[:, tile], act[:, tile], NT, HIGH)[0:1])
        lay_q.append(mm(s_all[:, cols], gpre[:, cols], NT, HIGH))
    lay_pos = mm(s_all, gpre[:, half:], NT, HIGH)
    ent_pos = mm(pos_pick, gh[:, nneg:], NT, HIGH)
    sco_pos = mm(scores8[:, nneg:], act[:, nneg:], NT, HIGH)[0:1]

    @pl.loop(0, edges // BLK)
    def _(j):
        srct[:, at_block(j)] = transposed(srcr[at_block(j), :])

    pltpu.make_async_copy(trecv.at[pl.ds(0, nodes - 1)], trecv.at[pl.ds(0, nodes - 1)], t_recv).wait()
    totals = jnp.sum(trecv[...], axis=0)
    loss_out[...] = pltpu.roll(totals, 128 - 2 * nq, 1) + pltpu.roll(totals, 128 - nq, 1) / totals
    ratio = jnp.where(lane128 < nq, part_row / totals, 0.0)
    ratios = [ratio[:, q : q + 1] for q in range(nq)]
    gs = jnp.concatenate([gs_neg[q * dd : (q + 1) * dd] * ratios[q] for q in range(nq)], axis=0) + gs_pos
    gs2 = split(gs, 2)

    ht = ht_neg * ratio + gh[:, nneg:]
    gq = mm(mq_w[...], ht, precision=HIGH) + hd_neg * ratio + hd_pos
    gquery = mm(qvt, ht, NT, HIGH)
    gent = ent_pos + sum(ent_q[q] * ratios[q] for q in range(nq))
    glayer = lay_pos + sum(lay_q[q] * ratios[q] for q in range(nq))
    gscore = sco_pos + sum(sco_q[q] * ratios[q] for q in range(nq))
    gq9 = split(jnp.concatenate([jnp.where(q_high == h, gq, 0.0) for h in range(3)], axis=0), 3)
    grel_q = join(mm(gq9, q_hot, NT), 3)

    @pl.loop(0, edges // WIDE)
    def _(j):
        c = at_block(j, WIDE)
        up = join(mm(gs2, odt[:, c]), 2) * srct[:, c]
        term = join(up, nq)
        high = jnp.concatenate([erel[pl.ds(4 * j + i, 1), :] for i in range(4)], axis=1) >> 8
        et6[:, c] = split(jnp.concatenate([jnp.where(high == h, term, 0.0) for h in range(3)], axis=0), 2)

    grel = grel_q + join(mm(et6[...], ort[...], NT), 2)

    gmat[...] = jnp.zeros_like(gmat)
    gmat[:, 0:256] = grel[:dd]
    gmat[:, 256:512] = grel[dd : 2 * dd]
    gmat[:, 512:768] = grel[2 * dd :]
    gmat[:, 544 : 544 + dd] = glayer
    gmat[:, 576 : 576 + hid] = gent
    gmat[:, 640 : 640 + hid] = gquery
    gmat[0:1, 704 : 704 + hid] = gscore
    for c in range(6):
        for r in range(4):
            rsrc[c * 4 + r] = gmat[r * 8 : r * 8 + 8, c * 128 : (c + 1) * 128]

    own = me < TILES

    @pl.loop(1, nodes)
    def _(k):
        to = (me + k) % nodes

        @pl.when(to < TILES)
        def _():
            pltpu.make_async_remote_copy(
                src_ref=rsrc.at[to],
                dst_ref=rsbuf.at[me],
                send_sem=r_send,
                recv_sem=r_recv,
                device_id=node_of(to),
                device_id_type=MESH,
            ).start()

    def wait_for(ref, sem):
        pltpu.make_async_copy(ref, ref, sem).wait()

    @pl.when(own)
    def _():
        rsbuf[me] = rsrc[me]
        wait_for(rsbuf.at[pl.ds(0, nodes - 1)], r_recv)
        zbuf[mz] = jnp.sum(rsbuf[...], axis=0)

        @pl.loop(1, zs)
        def _(k):
            pltpu.make_async_remote_copy(
                src_ref=zbuf.at[mz],
                dst_ref=zbuf.at[mz],
                send_sem=z_send,
                recv_sem=z_recv,
                device_id=(me, (mz + k) % zs),
                device_id_type=MESH,
            ).start()

        if zs > 1:
            wait_for(zbuf.at[pl.ds(0, zs - 1)], z_recv)
        ag[me] = jnp.sum(zbuf[...], axis=0)

        @pl.loop(1, nodes)
        def _(k):
            pltpu.make_async_remote_copy(
                src_ref=ag.at[me],
                dst_ref=ag.at[me],
                send_sem=a_send,
                recv_sem=a_recv,
                device_id=node_of((me + k) % nodes),
                device_id_type=MESH,
            ).start()

    new_out[...] = transposed(rows_of(new_all, nq, ent))

    wait_for(sbuf.at[chunk(0, nodes - 1)], s_send)
    wait_for(trecv.at[pl.ds(0, nodes - 1)], t_send)

    @pl.when(own)
    def _():
        wait_for(rsrc.at[pl.ds(0, TILES - 1)], r_send)
        if zs > 1:
            wait_for(zbuf.at[pl.ds(0, zs - 1)], z_send)
        wait_for(ag.at[pl.ds(0, TILES - 1)], a_recv)
        wait_for(rsbuf.at[pl.ds(0, nodes - 1)], a_send)

    @pl.when(jnp.logical_not(own))
    def _():
        wait_for(rsrc, r_send)
        wait_for(ag, a_recv)


def finish(
    new, loss, ag,
    new_o, loss_o, grel_o, glayer_o, gent_o, gquery_o, gscore_o,
    gmat, v_loss, v_rel, v_layer, v_ent, v_query, v_score, sem,
):
    first = pltpu.make_async_copy(new, new_o, sem.at[0])
    first.start()
    for c in range(6):
        for r in range(4):
            gmat[r * 8 : r * 8 + 8, c * 128 : (c + 1) * 128] = ag[c * 4 + r]
    nrel = v_rel.shape[1]
    dd, hid = v_ent.shape
    v_rel[...] = gmat[:, 0:nrel]
    copies = [pltpu.make_async_copy(v_rel, grel_o, sem.at[1])]
    v_layer[...] = gmat[:, 544 : 544 + dd]
    v_ent[...] = gmat[:, 576 : 576 + hid]
    v_query[...] = gmat[:, 640 : 640 + hid]
    v_score[...] = gmat[0:1, 704 : 704 + hid]
    v_loss[...] = loss[:, 0 : v_loss.shape[1]]
    pairs = ((v_layer, glayer_o), (v_ent, gent_o), (v_query, gquery_o), (v_score, gscore_o), (v_loss, loss_o))
    for i, (src, dst) in enumerate(pairs):
        copies.append(pltpu.make_async_copy(src, dst, sem.at[2 + i]))
    for copy in copies:
        copy.start()
    for copy in [first, *copies]:
        copy.wait()


def body(
    sizes,
    state_in, edge_src, edge_dst, edge_rel, edge_count, send_list, query_head, query_rel, pos_tail,
    neg_ids, rel_table, layer_weight, mlp_entity, mlp_query, score_weight,
):
    nodes, zs, nx, ny = sizes
    ent, width = state_in.shape
    nrel, dd = rel_table.shape
    hid = mlp_entity.shape[1]
    nq = width // dd
    edges = edge_src.shape[0]
    bnd = send_list.shape[2]
    sds = jax.ShapeDtypeStruct
    vmem = pl.BlockSpec(memory_space=pltpu.VMEM)
    hbm = pl.BlockSpec(memory_space=pltpu.HBM)
    dma = pltpu.SemaphoreType.DMA
    I32 = jnp.int32
    scratch = [
        pltpu.VMEM((ent, width), F32),
        pltpu.VMEM((ent + nodes * bnd, width), F32),
        pltpu.VMEM((nodes * bnd, width), F32),
        pltpu.VMEM((edges // 128, 128), I32),
        pltpu.VMEM((edges // 128, 128), I32),
        pltpu.VMEM(neg_ids.shape, I32),
        pltpu.VMEM((dd, nrel), F32),
        pltpu.VMEM((dd, dd), F32),
        pltpu.VMEM((dd, hid), F32),
        pltpu.VMEM((dd, hid), F32),
        pltpu.VMEM((1, hid), F32),
        pltpu.SMEM((edges,), I32),
        pltpu.SMEM((nodes, bnd), I32),
        pltpu.SMEM((1,), I32),
        pltpu.SMEM((nq,), I32),
        pltpu.SMEM((nq,), I32),
        pltpu.SMEM((nq,), I32),
        pltpu.VMEM((dd, 768), F32),
        pltpu.VMEM((9 * dd, 256), BF16),
        pltpu.VMEM((width, ent), F32),
        pltpu.VMEM((edges, width), F32),
        pltpu.VMEM((256, edges), BF16),
        pltpu.VMEM((ent, edges), BF16),
        pltpu.VMEM((edges, width), F32),
        pltpu.VMEM((width, edges), F32),
        pltpu.VMEM((edges, 3 * width), BF16),
        pltpu.VMEM((ent, 3 * width), F32),
        pltpu.VMEM((6 * dd, edges), BF16),
        pltpu.VMEM((1, 128), F32),
        pltpu.VMEM((nodes, 1, 128), F32),
        pltpu.VMEM((dd, 768), F32),
        pltpu.VMEM((TILES, 8, 128), F32),
        pltpu.VMEM((nodes, 8, 128), F32),
        pltpu.VMEM((zs, 8, 128), F32),
        dma((16,)), dma, dma, dma, dma, dma, dma, dma, dma, dma, dma,
    ]
    new, loss, ag = pl.pallas_call(
        functools.partial(kernel, (nodes, zs, nx, ny, nq * zs)),
        out_shape=(sds((ent, width), F32), sds((1, 128), F32), sds((TILES, 8, 128), F32)),
        in_specs=[hbm] * 15,
        out_specs=[vmem] * 3,
        scratch_shapes=scratch,
        compiler_params=pltpu.CompilerParams(
            collective_id=0, has_side_effects=True, vmem_limit_bytes=48 << 20
        ),
        name="layer",
    )(
        state_in,
        edge_src,
        edge_dst.reshape(edges // 128, 128),
        edge_rel.reshape(edges // 128, 128),
        send_list.reshape(nodes, bnd),
        neg_ids,
        rel_table.T,
        layer_weight,
        mlp_entity,
        mlp_query,
        score_weight.reshape(1, hid),
        edge_count,
        query_head,
        query_rel,
        pos_tail,
    )
    shapes = [(1, nq), (dd, nrel), (dd, dd), (dd, hid), (dd, hid), (1, hid)]
    new_state, loss, grel, glayer, gent, gquery, gscore = pl.pallas_call(
        finish,
        out_shape=[sds((ent, width), F32)] + [sds(s, F32) for s in shapes],
        in_specs=[vmem] * 3,
        out_specs=[hbm] * 7,
        scratch_shapes=[pltpu.VMEM((dd, 768), F32)] + [pltpu.VMEM(s, F32) for s in shapes] + [dma((7,))],
        name="finish",
    )(new, loss, ag)
    return new_state, loss.reshape(nq), grel.T, glayer, gent, gquery, gscore.reshape(hid)


def solution(mesh):
    nodes, zs = mesh.shape["nodes"], mesh.shape["queries"]
    nx = 4
    ny = nodes // (2 * nx)
    in_specs = (
        P("nodes", "queries"),
        P("nodes"),
        P("nodes"),
        P("nodes"),
        P("nodes"),
        P("nodes", None, None),
        P("queries"),
        P("queries"),
        P("queries"),
        P("queries", "nodes"),
        P(),
        P(),
        P(),
        P(),
        P(),
    )
    out_specs = (P("nodes", "queries"), P("queries"), P(), P(), P(), P(), P())
    return jax.shard_map(
        functools.partial(body, (nodes, zs, nx, ny)),
        mesh=mesh, in_specs=in_specs, out_specs=out_specs, check_vma=False,
    )
```

```python
import functools

import jax
import jax.numpy as jnp
from jax import lax
from jax.experimental import pallas as pl
from jax.experimental.pallas import tpu as pltpu
from jax.sharding import PartitionSpec as P

adversarial = 0.5
MESH = pl.DeviceIdType.MESH
HIGH = lax.Precision.HIGHEST
F32 = jnp.float32
BF16 = jnp.bfloat16
NT = (((1,), (1,)), ((), ()))
NN = (((1,), (0,)), ((), ()))
TILES = 24
BLK = 256
WIDE = 512


def mm(a, b, dims=NN, precision=None):
    return lax.dot_general(a, b, dims, precision=precision, preferred_element_type=F32)


def parts_of(x, terms):
    parts = []
    for i in range(terms):
        part = x.astype(BF16)
        parts.append(part)
        if i + 1 < terms:
            x = x - part.astype(F32)
    return parts


def split(x, terms, axis=0):
    return jnp.concatenate(parts_of(x, terms), axis=axis)


def join(y, terms):
    rows = y.shape[0] // terms
    out = y[:rows]
    for i in range(1, terms):
        out = out + y[i * rows : (i + 1) * rows]
    return out


def onehot(row, depth):
    ids = lax.broadcasted_iota(jnp.int32, (depth, row.shape[1]), 0)
    return jnp.where(ids == row, 1.0, 0.0).astype(BF16)


def lanes_of(x, queries, rows):
    return jnp.concatenate([x[q * rows : (q + 1) * rows] for q in range(queries)], axis=1)


def rows_of(x, queries, width):
    return jnp.concatenate([x[:, q * width : (q + 1) * width] for q in range(queries)], axis=0)


def transposed(x):
    r, c = x.shape
    return jnp.concatenate(
        [
            jnp.concatenate([x[i : i + 128, j : j + 128].T for i in range(0, r, 128)], axis=1)
            for j in range(0, c, 128)
        ],
        axis=0,
    )


def softplus(x):
    return jnp.maximum(x, 0.0) + jnp.log1p(jnp.exp(-jnp.abs(x)))


def sigmoid(x):
    return 1.0 / (1.0 + jnp.exp(-x))


def far_first(nx, ny):
    def away(d, n):
        return min(d, n - d)

    steps = [(dx, dy) for dy in range(ny) for dx in range(nx) if (dx, dy) != (0, 0)]
    return sorted(steps, key=lambda s: (-away(s[0], nx) - away(s[1], ny), s))


def kernel(
    cfg,
    h_state, h_esrc, h_edst, h_erel, h_slist, h_neg, h_rel, h_wl, h_me, h_mq, h_sw,
    h_count, h_head, h_qrel, h_tail,
    new_out, loss_out, ag,
    st_v, tab, sbuf, edst, erel, neg, relraw, wl, me_w, mq_w, sw,
    esrc, slist, ecount, qhead, qrel, ptail,
    relpad, rt9, stt_ref, relrow, ort, odt, srcr, srct, msg3, acc, et6,
    tsend, trecv, gmat, rsrc, rsbuf, zbuf,
    i_sem, s_send, s_recv, t_send, t_recv, r_send, r_recv, z_send, z_recv, a_send, a_recv,
):
    nodes, zs, nx, ny, queries_total = cfg
    me = lax.axis_index("nodes")
    mz = lax.axis_index("queries")
    chip = me // 2
    core = me % 2
    cx = chip % nx
    cy = chip // nx
    dd, hid = me_w.shape
    ent = h_state.shape[0]
    nq = h_state.shape[1] // dd
    edges = h_esrc.shape[0]
    bnd = h_slist.shape[1]
    blocks = edges // BLK
    nrel = relraw.shape[1]
    lane128 = lax.broadcasted_iota(jnp.int32, (1, 128), 1)

    def node_of(t):
        return (t, mz)

    loads = [
        pltpu.make_async_copy(src, dst, i_sem.at[i])
        for i, (src, dst) in enumerate(
            (
                (h_slist, slist), (h_state, st_v), (h_state, tab.at[pl.ds(0, ent)]), (h_rel, relraw), (h_erel, erel),
                (h_edst, edst), (h_esrc, esrc), (h_count, ecount), (h_qrel, qrel), (h_head, qhead),
                (h_tail, ptail), (h_neg, neg), (h_wl, wl), (h_me, me_w), (h_mq, mq_w), (h_sw, sw),
            )
        )
    ]
    for load in loads:
        load.start()
    barrier = pltpu.get_barrier_semaphore()

    @pl.loop(1, nodes)
    def _(k):
        pl.semaphore_signal(barrier, inc=1, device_id=node_of((me + k) % nodes), device_id_type=MESH)

    @pl.loop(1, zs)
    def _(k):
        pl.semaphore_signal(barrier, inc=1, device_id=(me, (mz + k) % zs), device_id_type=MESH)

    loads[0].wait()
    loads[1].wait()

    @pl.loop(0, nodes)
    def _(b):
        for k in range(bnd):
            sbuf[pl.ds(b * bnd + k, 1), :] = st_v[pl.ds(slist[b, k], 1), :]

    pl.semaphore_wait(barrier, nodes - 1 + zs - 1)

    def chunk(first, n=1):
        return pl.ds(pl.multiple_of(first * bnd, bnd), n * bnd)

    def send_rows(to):
        pltpu.make_async_remote_copy(
            src_ref=sbuf.at[chunk(to)],
            dst_ref=tab.at[pl.ds(pl.multiple_of(ent + me * bnd, bnd), bnd)],
            send_sem=s_send,
            recv_sem=s_recv,
            device_id=node_of(to),
            device_id_type=MESH,
        ).start()

    for dx, dy in far_first(nx, ny):
        there = 2 * (((cy + dy) % ny) * nx + (cx + dx) % nx)
        send_rows(there + core)
        send_rows(there + 1 - core)
    send_rows(2 * chip + 1 - core)
    tab[pl.ds(pl.multiple_of(ent + me * bnd, bnd), bnd), :] = sbuf[chunk(me), :]

    for load in loads[2:]:
        load.wait()
    stt_ref[...] = transposed(st_v[...])
    relpad[...] = jnp.zeros_like(relpad)
    relpad[:, 0:nrel] = relraw[...]
    rt9[...] = jnp.concatenate([split(relpad[:, h * 256 : (h + 1) * 256], 3) for h in range(3)], axis=0)

    def edge_row(ref, j):
        return jnp.concatenate([ref[pl.ds(2 * j, 1), :], ref[pl.ds(2 * j + 1, 1), :]], axis=1)

    def at_block(j, size=BLK):
        return pl.ds(pl.multiple_of(j * size, size), size)

    def relation(hot, high):
        got = mm(rt9[...], hot)
        out = jnp.zeros((dd, hot.shape[1]), F32)
        for h in range(3):
            out = jnp.where(high == h, join(got[h * 3 * dd : (h + 1) * 3 * dd], 3), out)
        return out

    lane256 = lax.broadcasted_iota(jnp.int32, (1, BLK), 1)

    @pl.loop(0, blocks)
    def _(j):
        row = edge_row(erel, j)
        hot = onehot(row & 255, 256)
        ort[:, at_block(j)] = hot
        relrow[at_block(j), :] = transposed(jnp.concatenate([relation(hot, row >> 8)] * nq, axis=0))
        dst = jnp.where(lane256 + j * BLK < ecount[0], edge_row(edst, j), -1)
        odt[:, at_block(j)] = onehot(dst, ent)

    qr = jnp.full((1, 128), -1, jnp.int32)
    for q in range(nq):
        qr = jnp.where(lane128 == q, qrel[q], qr)
    q_hot = onehot(qr & 255, 256)
    q_high = qr >> 8
    qvt = relation(q_hot, q_high)
    lane_ent = lax.broadcasted_iota(jnp.int32, (1, ent), 1)

    def local_of(g):
        return jnp.where(g // ent == me, g % ent, -1)

    heads = [jnp.where(lane_ent == local_of(qhead[q]), 1.0, 0.0) for q in range(nq)]
    tails = [jnp.where(lane_ent == local_of(ptail[q]), 1.0, 0.0) for q in range(nq)]
    head_term = jnp.concatenate([qvt[:, q : q + 1] * heads[q] for q in range(nq)], axis=1)
    qh = mm(mq_w[...].T, qvt, precision=HIGH)
    qh_wide = jnp.concatenate(
        [jnp.broadcast_to(qh[:, q : q + 1], (hid, 128)) for q in range(nq)] + [qh], axis=1
    )
    eye = lax.broadcasted_iota(jnp.int32, (hid, hid), 0) == lax.broadcasted_iota(jnp.int32, (hid, hid), 1)
    swc = jnp.sum(jnp.where(eye, sw[...], 0.0), axis=1, keepdims=True)
    acc[...] = jnp.zeros_like(acc)

    pltpu.make_async_copy(sbuf.at[chunk(0, nodes - 1)], sbuf.at[chunk(0, nodes - 1)], s_recv).wait()

    def gather(j):
        for u in range(BLK):
            srcr[pl.ds(j * BLK + u, 1), :] = tab[pl.ds(esrc[j * BLK + u], 1), :]
        msg3[at_block(j), :] = split(srcr[at_block(j), :] * relrow[at_block(j), :], 3, axis=1)

    def scatter(j):
        acc[...] += mm(odt[:, at_block(j)], msg3[at_block(j), :])

    gather(0)

    @pl.loop(1, blocks)
    def _(j):
        scatter(j - 1)
        gather(j)

    scatter(blocks - 1)
    width = nq * dd
    summed = acc[:, 0:width] + acc[:, width : 2 * width] + acc[:, 2 * width : 3 * width]
    s_all = lanes_of(transposed(summed), nq, dd) + head_term
    pre = mm(wl[...].T, s_all, precision=HIGH)
    new_all = lanes_of(stt_ref[...], nq, dd) + jnp.maximum(pre, 0.0)

    picks = []
    hots = []
    pos_pick = jnp.zeros((dd, 128), F32)
    is_pos = lane128 < 0
    for q in range(nq):
        mine = new_all[:, q * ent : (q + 1) * ent]
        ids = neg[q : q + 1, :]
        low = jnp.broadcast_to(ids & 127, (dd, 128))
        out = jnp.zeros((dd, 128), F32)
        for b in range(ent // 128):
            got = jnp.take_along_axis(
                mine[:, b * 128 : (b + 1) * 128], low, axis=1, mode="promise_in_bounds"
            )
            out = jnp.where((ids >> 7) == b, got, out)
        picks.append(out)
        hots.append(onehot(ids, ent))
        pos_pick = jnp.where(lane128 == q, jnp.sum(mine * tails[q], axis=1, keepdims=True), pos_pick)
        is_pos = is_pos | ((lane128 == q) & (ptail[q] // ent == me))
    picked = jnp.concatenate(picks + [pos_pick], axis=1)
    pre_h = mm(me_w[...].T, picked, precision=HIGH) + qh_wide
    act = jnp.maximum(pre_h, 0.0)
    score = jnp.sum(act * swc, axis=0, keepdims=True)
    nneg = nq * 128
    s_neg = rows_of(score[:, :nneg], nq, 128)
    s_pos = score[:, nneg:]
    weight = jnp.exp(adversarial * s_neg)
    part_total = jnp.sum(weight, axis=1, keepdims=True)
    part_weighted = jnp.sum(weight * softplus(s_neg), axis=1, keepdims=True)
    sub = lax.broadcasted_iota(jnp.int32, (nq, 128), 0)
    lanes = lax.broadcasted_iota(jnp.int32, (nq, 128), 1)

    def row_of(col, first):
        return jnp.sum(jnp.where(lanes == sub + first, col, 0.0), axis=0, keepdims=True)

    part_row = row_of(part_total, 0)
    pos_terms = jnp.where(is_pos, softplus(-s_pos), 0.0)
    line = part_row + row_of(part_weighted, nq) + pltpu.roll(pos_terms, 2 * nq, 1)
    tsend[...] = line
    trecv[me] = line

    @pl.loop(1, nodes)
    def _(k):
        pltpu.make_async_remote_copy(
            src_ref=tsend,
            dst_ref=trecv.at[me],
            send_sem=t_send,
            recv_sem=t_recv,
            device_id=node_of((me + k) % nodes),
            device_id_type=MESH,
        ).start()

    safe = jnp.where(part_total > 0, part_total, 1.0)
    c_neg = weight / safe * sigmoid(s_neg) / queries_total
    c_pos = jnp.where(is_pos, sigmoid(s_pos) - 1.0, 0.0) / queries_total
    coef = jnp.concatenate([c_neg[q : q + 1] for q in range(nq)] + [c_pos], axis=1)
    gh = coef * swc * jnp.where(pre_h > 0, 1.0, 0.0)
    gp = mm(me_w[...], gh, precision=HIGH)
    gc_neg = jnp.concatenate(
        [join(mm(split(gp[:, q * 128 : (q + 1) * 128], 3), hots[q], NT), 3) for q in range(nq)], axis=1
    )
    gc_pos = jnp.concatenate([gp[:, nneg + q : nneg + q + 1] * tails[q] for q in range(nq)], axis=1)
    gpre = jnp.concatenate([jnp.where(pre > 0, gc_neg, 0.0), jnp.where(pre > 0, gc_pos, 0.0)], axis=1)
    gsum = mm(wl[...], gpre, precision=HIGH)
    half = nq * ent
    gs_neg = rows_of(gsum[:, :half], nq, ent)
    gs_pos = rows_of(gsum[:, half:], nq, ent)

    ht_neg = jnp.zeros((hid, 128), F32)
    hd_neg = jnp.zeros((dd, 128), F32)
    hd_pos = jnp.zeros((dd, 128), F32)
    scores8 = jnp.broadcast_to(coef, (8, nneg + 128))
    ent_q, lay_q, sco_q = [], [], []
    lay_pos = jnp.zeros((dd, dd), F32)
    for q in range(nq):
        tile = slice(q * 128, (q + 1) * 128)
        cols = slice(q * ent, (q + 1) * ent)
        here = lane128 == q
        ht_neg = jnp.where(here, jnp.sum(gh[:, tile], axis=1, keepdims=True), ht_neg)
        hd_neg = jnp.where(here, jnp.sum(gsum[:, cols] * heads[q], axis=1, keepdims=True), hd_neg)
        g_p = gsum[:, half + q * ent : half + (q + 1) * ent]
        hd_pos = jnp.where(here, jnp.sum(g_p * heads[q], axis=1, keepdims=True), hd_pos)
        ent_q.append(mm(picked[:, tile], gh[:, tile], NT, HIGH))
        sco_q.append(mm(scores8[:, tile], act[:, tile], NT, HIGH)[0:1])
        lay_q.append(mm(s_all[:, cols], gpre[:, cols], NT, HIGH))
    lay_pos = mm(s_all, gpre[:, half:], NT, HIGH)
    ent_pos = mm(pos_pick, gh[:, nneg:], NT, HIGH)
    sco_pos = mm(scores8[:, nneg:], act[:, nneg:], NT, HIGH)[0:1]

    @pl.loop(0, edges // BLK)
    def _(j):
        srct[:, at_block(j)] = transposed(srcr[at_block(j), :])

    pltpu.make_async_copy(trecv.at[pl.ds(0, nodes - 1)], trecv.at[pl.ds(0, nodes - 1)], t_recv).wait()
    totals = jnp.sum(trecv[...], axis=0)
    loss_out[...] = pltpu.roll(totals, 128 - 2 * nq, 1) + pltpu.roll(totals, 128 - nq, 1) / totals
    ratio = jnp.where(lane128 < nq, part_row / totals, 0.0)
    ratios = [ratio[:, q : q + 1] for q in range(nq)]
    gs = jnp.concatenate([gs_neg[q * dd : (q + 1) * dd] * ratios[q] for q in range(nq)], axis=0) + gs_pos
    gs2 = split(gs, 2)

    ht = ht_neg * ratio + gh[:, nneg:]
    gq = mm(mq_w[...], ht, precision=HIGH) + hd_neg * ratio + hd_pos
    gquery = mm(qvt, ht, NT, HIGH)
    gent = ent_pos + sum(ent_q[q] * ratios[q] for q in range(nq))
    glayer = lay_pos + sum(lay_q[q] * ratios[q] for q in range(nq))
    gscore = sco_pos + sum(sco_q[q] * ratios[q] for q in range(nq))
    gq9 = split(jnp.concatenate([jnp.where(q_high == h, gq, 0.0) for h in range(3)], axis=0), 3)
    grel_q = join(mm(gq9, q_hot, NT), 3)

    @pl.loop(0, edges // WIDE)
    def _(j):
        c = at_block(j, WIDE)
        up = join(mm(gs2, odt[:, c]), 2) * srct[:, c]
        term = join(up, nq)
        high = jnp.concatenate([erel[pl.ds(4 * j + i, 1), :] for i in range(4)], axis=1) >> 8
        et6[:, c] = split(jnp.concatenate([jnp.where(high == h, term, 0.0) for h in range(3)], axis=0), 2)

    grel = grel_q + join(mm(et6[...], ort[...], NT), 2)

    gmat[...] = jnp.zeros_like(gmat)
    gmat[:, 0:256] = grel[:dd]
    gmat[:, 256:512] = grel[dd : 2 * dd]
    gmat[:, 512:768] = grel[2 * dd :]
    gmat[:, 544 : 544 + dd] = glayer
    gmat[:, 576 : 576 + hid] = gent
    gmat[:, 640 : 640 + hid] = gquery
    gmat[0:1, 704 : 704 + hid] = gscore
    for c in range(6):
        for r in range(4):
            rsrc[c * 4 + r] = gmat[r * 8 : r * 8 + 8, c * 128 : (c + 1) * 128]

    own = me < TILES

    @pl.loop(1, nodes)
    def _(k):
        to = (me + k) % nodes

        @pl.when(to < TILES)
        def _():
            pltpu.make_async_remote_copy(
                src_ref=rsrc.at[to],
                dst_ref=rsbuf.at[me],
                send_sem=r_send,
                recv_sem=r_recv,
                device_id=node_of(to),
                device_id_type=MESH,
            ).start()

    def wait_for(ref, sem):
        pltpu.make_async_copy(ref, ref, sem).wait()

    @pl.when(own)
    def _():
        rsbuf[me] = rsrc[me]
        wait_for(rsbuf.at[pl.ds(0, nodes - 1)], r_recv)
        zbuf[mz] = jnp.sum(rsbuf[...], axis=0)

        @pl.loop(1, zs)
        def _(k):
            pltpu.make_async_remote_copy(
                src_ref=zbuf.at[mz],
                dst_ref=zbuf.at[mz],
                send_sem=z_send,
                recv_sem=z_recv,
                device_id=(me, (mz + k) % zs),
                device_id_type=MESH,
            ).start()

        if zs > 1:
            wait_for(zbuf.at[pl.ds(0, zs - 1)], z_recv)
        ag[me] = jnp.sum(zbuf[...], axis=0)

        @pl.loop(1, nodes)
        def _(k):
            pltpu.make_async_remote_copy(
                src_ref=ag.at[me],
                dst_ref=ag.at[me],
                send_sem=a_send,
                recv_sem=a_recv,
                device_id=node_of((me + k) % nodes),
                device_id_type=MESH,
            ).start()

    new_out[...] = transposed(rows_of(new_all, nq, ent))

    wait_for(sbuf.at[chunk(0, nodes - 1)], s_send)
    wait_for(trecv.at[pl.ds(0, nodes - 1)], t_send)

    @pl.when(own)
    def _():
        wait_for(rsrc.at[pl.ds(0, TILES - 1)], r_send)
        if zs > 1:
            wait_for(zbuf.at[pl.ds(0, zs - 1)], z_send)
        wait_for(ag.at[pl.ds(0, TILES - 1)], a_recv)
        wait_for(rsbuf.at[pl.ds(0, nodes - 1)], a_send)

    @pl.when(jnp.logical_not(own))
    def _():
        wait_for(rsrc, r_send)
        wait_for(ag, a_recv)


def finish(
    new, loss, ag,
    new_o, loss_o, grel_o, glayer_o, gent_o, gquery_o, gscore_o,
    gmat, v_loss, v_rel, v_layer, v_ent, v_query, v_score, sem,
):
    first = pltpu.make_async_copy(new, new_o, sem.at[0])
    first.start()
    for c in range(6):
        for r in range(4):
            gmat[r * 8 : r * 8 + 8, c * 128 : (c + 1) * 128] = ag[c * 4 + r]
    nrel = v_rel.shape[1]
    dd, hid = v_ent.shape
    v_rel[...] = gmat[:, 0:nrel]
    copies = [pltpu.make_async_copy(v_rel, grel_o, sem.at[1])]
    v_layer[...] = gmat[:, 544 : 544 + dd]
    v_ent[...] = gmat[:, 576 : 576 + hid]
    v_query[...] = gmat[:, 640 : 640 + hid]
    v_score[...] = gmat[0:1, 704 : 704 + hid]
    v_loss[...] = loss[:, 0 : v_loss.shape[1]]
    pairs = ((v_layer, glayer_o), (v_ent, gent_o), (v_query, gquery_o), (v_score, gscore_o), (v_loss, loss_o))
    for i, (src, dst) in enumerate(pairs):
        copies.append(pltpu.make_async_copy(src, dst, sem.at[2 + i]))
    for copy in copies:
        copy.start()
    for copy in [first, *copies]:
        copy.wait()


def body(
    sizes,
    state_in, edge_src, edge_dst, edge_rel, edge_count, send_list, query_head, query_rel, pos_tail,
    neg_ids, rel_table, layer_weight, mlp_entity, mlp_query, score_weight,
):
    nodes, zs, nx, ny = sizes
    ent, width = state_in.shape
    nrel, dd = rel_table.shape
    hid = mlp_entity.shape[1]
    nq = width // dd
    edges = edge_src.shape[0]
    bnd = send_list.shape[2]
    sds = jax.ShapeDtypeStruct
    vmem = pl.BlockSpec(memory_space=pltpu.VMEM)
    hbm = pl.BlockSpec(memory_space=pltpu.HBM)
    dma = pltpu.SemaphoreType.DMA
    I32 = jnp.int32
    scratch = [
        pltpu.VMEM((ent, width), F32),
        pltpu.VMEM((ent + nodes * bnd, width), F32),
        pltpu.VMEM((nodes * bnd, width), F32),
        pltpu.VMEM((edges // 128, 128), I32),
        pltpu.VMEM((edges // 128, 128), I32),
        pltpu.VMEM(neg_ids.shape, I32),
        pltpu.VMEM((dd, nrel), F32),
        pltpu.VMEM((dd, dd), F32),
        pltpu.VMEM((dd, hid), F32),
        pltpu.VMEM((dd, hid), F32),
        pltpu.VMEM((1, hid), F32),
        pltpu.SMEM((edges,), I32),
        pltpu.SMEM((nodes, bnd), I32),
        pltpu.SMEM((1,), I32),
        pltpu.SMEM((nq,), I32),
        pltpu.SMEM((nq,), I32),
        pltpu.SMEM((nq,), I32),
        pltpu.VMEM((dd, 768), F32),
        pltpu.VMEM((9 * dd, 256), BF16),
        pltpu.VMEM((width, ent), F32),
        pltpu.VMEM((edges, width), F32),
        pltpu.VMEM((256, edges), BF16),
        pltpu.VMEM((ent, edges), BF16),
        pltpu.VMEM((edges, width), F32),
        pltpu.VMEM((width, edges), F32),
        pltpu.VMEM((edges, 3 * width), BF16),
        pltpu.VMEM((ent, 3 * width), F32),
        pltpu.VMEM((6 * dd, edges), BF16),
        pltpu.VMEM((1, 128), F32),
        pltpu.VMEM((nodes, 1, 128), F32),
        pltpu.VMEM((dd, 768), F32),
        pltpu.VMEM((TILES, 8, 128), F32),
        pltpu.VMEM((nodes, 8, 128), F32),
        pltpu.VMEM((zs, 8, 128), F32),
        dma((16,)), dma, dma, dma, dma, dma, dma, dma, dma, dma, dma,
    ]
    new, loss, ag = pl.pallas_call(
        functools.partial(kernel, (nodes, zs, nx, ny, nq * zs)),
        out_shape=(sds((ent, width), F32), sds((1, 128), F32), sds((TILES, 8, 128), F32)),
        in_specs=[hbm] * 15,
        out_specs=[vmem] * 3,
        scratch_shapes=scratch,
        compiler_params=pltpu.CompilerParams(
            collective_id=0, has_side_effects=True
        ),
        name="layer",
    )(
        state_in,
        edge_src,
        edge_dst.reshape(edges // 128, 128),
        edge_rel.reshape(edges // 128, 128),
        send_list.reshape(nodes, bnd),
        neg_ids,
        rel_table.T,
        layer_weight,
        mlp_entity,
        mlp_query,
        score_weight.reshape(1, hid),
        edge_count,
        query_head,
        query_rel,
        pos_tail,
    )
    shapes = [(1, nq), (dd, nrel), (dd, dd), (dd, hid), (dd, hid), (1, hid)]
    new_state, loss, grel, glayer, gent, gquery, gscore = pl.pallas_call(
        finish,
        out_shape=[sds((ent, width), F32)] + [sds(s, F32) for s in shapes],
        in_specs=[vmem] * 3,
        out_specs=[hbm] * 7,
        scratch_shapes=[pltpu.VMEM((dd, 768), F32)] + [pltpu.VMEM(s, F32) for s in shapes] + [dma((7,))],
        name="finish",
    )(new, loss, ag)
    return new_state, loss.reshape(nq), grel.T, glayer, gent, gquery, gscore.reshape(hid)


def solution(mesh):
    nodes, zs = mesh.shape["nodes"], mesh.shape["queries"]
    nx = 4
    ny = nodes // (2 * nx)
    in_specs = (
        P("nodes", "queries"),
        P("nodes"),
        P("nodes"),
        P("nodes"),
        P("nodes"),
        P("nodes", None, None),
        P("queries"),
        P("queries"),
        P("queries"),
        P("queries", "nodes"),
        P(),
        P(),
        P(),
        P(),
        P(),
    )
    out_specs = (P("nodes", "queries"), P("queries"), P(), P(), P(), P(), P())
    return jax.shard_map(
        functools.partial(body, (nodes, zs, nx, ny)),
        mesh=mesh, in_specs=in_specs, out_specs=out_specs, check_vma=False,
    )
```

```python
import functools

import jax
import jax.numpy as jnp
from jax import lax
from jax.experimental import pallas as pl
from jax.experimental.pallas import tpu as pltpu
from jax.sharding import PartitionSpec as P

adversarial = 0.5
MESH = pl.DeviceIdType.MESH
HIGH = lax.Precision.HIGHEST
F32 = jnp.float32
BF16 = jnp.bfloat16
NT = (((1,), (1,)), ((), ()))
NN = (((1,), (0,)), ((), ()))
TILES = 24
BLK = 256
WIDE = 512


def mm(a, b, dims=NN, precision=None):
    return lax.dot_general(a, b, dims, precision=precision, preferred_element_type=F32)


def parts_of(x, terms):
    parts = []
    for i in range(terms):
        part = x.astype(BF16)
        parts.append(part)
        if i + 1 < terms:
            x = x - part.astype(F32)
    return parts


def split(x, terms, axis=0):
    return jnp.concatenate(parts_of(x, terms), axis=axis)


def join(y, terms):
    rows = y.shape[0] // terms
    out = y[:rows]
    for i in range(1, terms):
        out = out + y[i * rows : (i + 1) * rows]
    return out


def onehot(row, depth):
    ids = lax.broadcasted_iota(jnp.int32, (depth, row.shape[1]), 0)
    return jnp.where(ids == row, 1.0, 0.0).astype(BF16)


def lanes_of(x, queries, rows):
    return jnp.concatenate([x[q * rows : (q + 1) * rows] for q in range(queries)], axis=1)


def rows_of(x, queries, width):
    return jnp.concatenate([x[:, q * width : (q + 1) * width] for q in range(queries)], axis=0)


def transposed(x):
    r, c = x.shape
    return jnp.concatenate(
        [
            jnp.concatenate([x[i : i + 128, j : j + 128].T for i in range(0, r, 128)], axis=1)
            for j in range(0, c, 128)
        ],
        axis=0,
    )


def softplus(x):
    return jnp.maximum(x, 0.0) + jnp.log1p(jnp.exp(-jnp.abs(x)))


def sigmoid(x):
    return 1.0 / (1.0 + jnp.exp(-x))


def far_first(nx, ny):
    def away(d, n):
        return min(d, n - d)

    steps = [(dx, dy) for dy in range(ny) for dx in range(nx) if (dx, dy) != (0, 0)]
    return sorted(steps, key=lambda s: (-away(s[0], nx) - away(s[1], ny), s))


def kernel(
    cfg,
    h_state, h_esrc, h_edst, h_erel, h_slist, h_neg, h_rel, h_wl, h_me, h_mq, h_sw,
    h_count, h_head, h_qrel, h_tail,
    new_out, loss_out, ag,
    st_v, tab, sbuf, edst, erel, neg, relraw, wl, me_w, mq_w, sw,
    esrc, slist, ecount, qhead, qrel, ptail,
    relpad, rt9, stt_ref, relrow, ort, odt, srcr, srct, msg3, acc, et6,
    tsend, trecv, gmat, rsrc, rsbuf, zbuf,
    i_sem, s_send, s_recv, t_send, t_recv, r_send, r_recv, z_send, z_recv, a_send, a_recv,
):
    nodes, zs, nx, ny, queries_total = cfg
    me = lax.axis_index("nodes")
    mz = lax.axis_index("queries")
    chip = me // 2
    core = me % 2
    cx = chip % nx
    cy = chip // nx
    dd, hid = me_w.shape
    ent = h_state.shape[0]
    nq = h_state.shape[1] // dd
    edges = h_esrc.shape[0]
    bnd = h_slist.shape[1]
    blocks = edges // BLK
    nrel = relraw.shape[1]
    lane128 = lax.broadcasted_iota(jnp.int32, (1, 128), 1)

    def node_of(t):
        return (t, mz)

    loads = [
        pltpu.make_async_copy(src, dst, i_sem.at[i])
        for i, (src, dst) in enumerate(
            (
                (h_slist, slist), (h_state, st_v), (h_state, tab.at[pl.ds(0, ent)]), (h_rel, relraw), (h_erel, erel),
                (h_edst, edst), (h_esrc, esrc), (h_count, ecount), (h_qrel, qrel), (h_head, qhead),
                (h_tail, ptail), (h_neg, neg), (h_wl, wl), (h_me, me_w), (h_mq, mq_w), (h_sw, sw),
            )
        )
    ]
    for load in loads:
        load.start()
    barrier = pltpu.get_barrier_semaphore()

    @pl.loop(1, nodes)
    def _(k):
        pl.semaphore_signal(barrier, inc=1, device_id=node_of((me + k) % nodes), device_id_type=MESH)

    @pl.loop(1, zs)
    def _(k):
        pl.semaphore_signal(barrier, inc=1, device_id=(me, (mz + k) % zs), device_id_type=MESH)

    loads[0].wait()
    loads[1].wait()

    for b in range(nodes):
        for k in range(bnd):
            e = b * bnd + k
            sbuf[e : e + 1, :] = st_v[pl.ds(slist[b, k], 1), :]

    pl.semaphore_wait(barrier, nodes - 1 + zs - 1)

    def peers():
        for dx, dy in far_first(nx, ny):
            there = 2 * (((cy + dy) % ny) * nx + (cx + dx) % nx)
            yield there + core
            yield there + 1 - core
        yield 2 * chip + 1 - core

    def chunk(first, n=1):
        return pl.ds(pl.multiple_of(first * bnd, bnd), n * bnd)

    def send_rows(to):
        pltpu.make_async_remote_copy(
            src_ref=sbuf.at[chunk(to)],
            dst_ref=tab.at[pl.ds(pl.multiple_of(ent + me * bnd, bnd), bnd)],
            send_sem=s_send,
            recv_sem=s_recv,
            device_id=node_of(to),
            device_id_type=MESH,
        ).start()

    for to in peers():
        send_rows(to)
    tab[pl.ds(pl.multiple_of(ent + me * bnd, bnd), bnd), :] = sbuf[chunk(me), :]

    for load in loads[2:]:
        load.wait()
    stt_ref[...] = transposed(st_v[...])
    relpad[...] = jnp.zeros_like(relpad)
    relpad[:, 0:nrel] = relraw[...]
    rt9[...] = jnp.concatenate([split(relpad[:, h * 256 : (h + 1) * 256], 3) for h in range(3)], axis=0)

    def edge_row(ref, j):
        return jnp.concatenate([ref[pl.ds(2 * j, 1), :], ref[pl.ds(2 * j + 1, 1), :]], axis=1)

    def at_block(j, size=BLK):
        if isinstance(j, int):
            return slice(j * size, (j + 1) * size)
        return pl.ds(pl.multiple_of(j * size, size), size)

    def relation(hot, high):
        got = mm(rt9[...], hot)
        out = jnp.zeros((dd, hot.shape[1]), F32)
        for h in range(3):
            out = jnp.where(high == h, join(got[h * 3 * dd : (h + 1) * 3 * dd], 3), out)
        return out

    lane256 = lax.broadcasted_iota(jnp.int32, (1, BLK), 1)

    @pl.loop(0, blocks)
    def _(j):
        row = edge_row(erel, j)
        hot = onehot(row & 255, 256)
        ort[:, at_block(j)] = hot
        relrow[at_block(j), :] = transposed(jnp.concatenate([relation(hot, row >> 8)] * nq, axis=0))
        dst = jnp.where(lane256 + j * BLK < ecount[0], edge_row(edst, j), -1)
        odt[:, at_block(j)] = onehot(dst, ent)

    qr = jnp.full((1, 128), -1, jnp.int32)
    for q in range(nq):
        qr = jnp.where(lane128 == q, qrel[q], qr)
    q_hot = onehot(qr & 255, 256)
    q_high = qr >> 8
    qvt = relation(q_hot, q_high)
    lane_ent = lax.broadcasted_iota(jnp.int32, (1, ent), 1)

    def local_of(g):
        return jnp.where(g // ent == me, g % ent, -1)

    heads = [jnp.where(lane_ent == local_of(qhead[q]), 1.0, 0.0) for q in range(nq)]
    tails = [jnp.where(lane_ent == local_of(ptail[q]), 1.0, 0.0) for q in range(nq)]
    head_term = jnp.concatenate([qvt[:, q : q + 1] * heads[q] for q in range(nq)], axis=1)
    qh = mm(mq_w[...].T, qvt, precision=HIGH)
    qh_wide = jnp.concatenate(
        [jnp.broadcast_to(qh[:, q : q + 1], (hid, 128)) for q in range(nq)] + [qh], axis=1
    )
    eye = lax.broadcasted_iota(jnp.int32, (hid, hid), 0) == lax.broadcasted_iota(jnp.int32, (hid, hid), 1)
    swc = jnp.sum(jnp.where(eye, sw[...], 0.0), axis=1, keepdims=True)
    acc[...] = jnp.zeros_like(acc)

    pltpu.make_async_copy(sbuf.at[chunk(0, nodes - 1)], sbuf.at[chunk(0, nodes - 1)], s_recv).wait()

    def gather(j):
        for u in range(BLK):
            e = j * BLK + u
            srcr[pl.ds(e, 1), :] = tab[pl.ds(esrc[e], 1), :]
        msg3[at_block(j), :] = split(srcr[at_block(j), :] * relrow[at_block(j), :], 3, axis=1)

    def scatter(j):
        acc[...] += mm(odt[:, at_block(j)], msg3[at_block(j), :])

    gather(0)

    @pl.loop(0, (blocks - 1) // 5)
    def _(t):
        for i in range(5):
            scatter(5 * t + i)
            gather(5 * t + i + 1)

    scatter(blocks - 1)
    width = nq * dd
    summed = acc[:, 0:width] + acc[:, width : 2 * width] + acc[:, 2 * width : 3 * width]
    s_all = lanes_of(transposed(summed), nq, dd) + head_term
    pre = mm(wl[...].T, s_all, precision=HIGH)
    new_all = lanes_of(stt_ref[...], nq, dd) + jnp.maximum(pre, 0.0)

    picks = []
    hots = []
    pos_pick = jnp.zeros((dd, 128), F32)
    is_pos = lane128 < 0
    for q in range(nq):
        mine = new_all[:, q * ent : (q + 1) * ent]
        ids = neg[q : q + 1, :]
        low = jnp.broadcast_to(ids & 127, (dd, 128))
        out = jnp.zeros((dd, 128), F32)
        for b in range(ent // 128):
            got = jnp.take_along_axis(
                mine[:, b * 128 : (b + 1) * 128], low, axis=1, mode="promise_in_bounds"
            )
            out = jnp.where((ids >> 7) == b, got, out)
        picks.append(out)
        hots.append(onehot(ids, ent))
        pos_pick = jnp.where(lane128 == q, jnp.sum(mine * tails[q], axis=1, keepdims=True), pos_pick)
        is_pos = is_pos | ((lane128 == q) & (ptail[q] // ent == me))
    picked = jnp.concatenate(picks + [pos_pick], axis=1)
    pre_h = mm(me_w[...].T, picked, precision=HIGH) + qh_wide
    act = jnp.maximum(pre_h, 0.0)
    score = jnp.sum(act * swc, axis=0, keepdims=True)
    nneg = nq * 128
    s_neg = rows_of(score[:, :nneg], nq, 128)
    s_pos = score[:, nneg:]
    weight = jnp.exp(adversarial * s_neg)
    part_total = jnp.sum(weight, axis=1, keepdims=True)
    part_weighted = jnp.sum(weight * softplus(s_neg), axis=1, keepdims=True)
    sub = lax.broadcasted_iota(jnp.int32, (nq, 128), 0)
    lanes = lax.broadcasted_iota(jnp.int32, (nq, 128), 1)

    def row_of(col, first):
        return jnp.sum(jnp.where(lanes == sub + first, col, 0.0), axis=0, keepdims=True)

    part_row = row_of(part_total, 0)
    pos_terms = jnp.where(is_pos, softplus(-s_pos), 0.0)
    line = part_row + row_of(part_weighted, nq) + pltpu.roll(pos_terms, 2 * nq, 1)
    tsend[...] = line
    trecv[me] = line
    for to in peers():
        pltpu.make_async_remote_copy(
            src_ref=tsend,
            dst_ref=trecv.at[me],
            send_sem=t_send,
            recv_sem=t_recv,
            device_id=node_of(to),
            device_id_type=MESH,
        ).start()

    safe = jnp.where(part_total > 0, part_total, 1.0)
    c_neg = weight / safe * sigmoid(s_neg) / queries_total
    c_pos = jnp.where(is_pos, sigmoid(s_pos) - 1.0, 0.0) / queries_total
    coef = jnp.concatenate([c_neg[q : q + 1] for q in range(nq)] + [c_pos], axis=1)
    gh = coef * swc * jnp.where(pre_h > 0, 1.0, 0.0)
    gp = mm(me_w[...], gh, precision=HIGH)
    gc_neg = jnp.concatenate(
        [join(mm(split(gp[:, q * 128 : (q + 1) * 128], 3), hots[q], NT), 3) for q in range(nq)], axis=1
    )
    gc_pos = jnp.concatenate([gp[:, nneg + q : nneg + q + 1] * tails[q] for q in range(nq)], axis=1)
    gpre = jnp.concatenate([jnp.where(pre > 0, gc_neg, 0.0), jnp.where(pre > 0, gc_pos, 0.0)], axis=1)
    gsum = mm(wl[...], gpre, precision=HIGH)
    half = nq * ent
    gs_neg = rows_of(gsum[:, :half], nq, ent)
    gs_pos = rows_of(gsum[:, half:], nq, ent)

    ht_neg = jnp.zeros((hid, 128), F32)
    hd_neg = jnp.zeros((dd, 128), F32)
    hd_pos = jnp.zeros((dd, 128), F32)
    scores8 = jnp.broadcast_to(coef, (8, nneg + 128))
    ent_q, lay_q, sco_q = [], [], []
    lay_pos = jnp.zeros((dd, dd), F32)
    for q in range(nq):
        tile = slice(q * 128, (q + 1) * 128)
        cols = slice(q * ent, (q + 1) * ent)
        here = lane128 == q
        ht_neg = jnp.where(here, jnp.sum(gh[:, tile], axis=1, keepdims=True), ht_neg)
        hd_neg = jnp.where(here, jnp.sum(gsum[:, cols] * heads[q], axis=1, keepdims=True), hd_neg)
        g_p = gsum[:, half + q * ent : half + (q + 1) * ent]
        hd_pos = jnp.where(here, jnp.sum(g_p * heads[q], axis=1, keepdims=True), hd_pos)
        ent_q.append(mm(picked[:, tile], gh[:, tile], NT, HIGH))
        sco_q.append(mm(scores8[:, tile], act[:, tile], NT, HIGH)[0:1])
        lay_q.append(mm(s_all[:, cols], gpre[:, cols], NT, HIGH))
    lay_pos = mm(s_all, gpre[:, half:], NT, HIGH)
    ent_pos = mm(pos_pick, gh[:, nneg:], NT, HIGH)
    sco_pos = mm(scores8[:, nneg:], act[:, nneg:], NT, HIGH)[0:1]

    @pl.loop(0, edges // BLK)
    def _(j):
        srct[:, at_block(j)] = transposed(srcr[at_block(j), :])

    pltpu.make_async_copy(trecv.at[pl.ds(0, nodes - 1)], trecv.at[pl.ds(0, nodes - 1)], t_recv).wait()
    totals = jnp.sum(trecv[...], axis=0)
    loss_out[...] = pltpu.roll(totals, 128 - 2 * nq, 1) + pltpu.roll(totals, 128 - nq, 1) / totals
    ratio = jnp.where(lane128 < nq, part_row / totals, 0.0)
    ratios = [ratio[:, q : q + 1] for q in range(nq)]
    gs = jnp.concatenate([gs_neg[q * dd : (q + 1) * dd] * ratios[q] for q in range(nq)], axis=0) + gs_pos
    gs2 = split(gs, 2)

    ht = ht_neg * ratio + gh[:, nneg:]
    gq = mm(mq_w[...], ht, precision=HIGH) + hd_neg * ratio + hd_pos
    gquery = mm(qvt, ht, NT, HIGH)
    gent = ent_pos + sum(ent_q[q] * ratios[q] for q in range(nq))
    glayer = lay_pos + sum(lay_q[q] * ratios[q] for q in range(nq))
    gscore = sco_pos + sum(sco_q[q] * ratios[q] for q in range(nq))
    gq9 = split(jnp.concatenate([jnp.where(q_high == h, gq, 0.0) for h in range(3)], axis=0), 3)
    grel_q = join(mm(gq9, q_hot, NT), 3)

    @pl.loop(0, edges // WIDE)
    def _(j):
        c = at_block(j, WIDE)
        up = join(mm(gs2, odt[:, c]), 2) * srct[:, c]
        term = join(up, nq)
        high = jnp.concatenate([erel[pl.ds(4 * j + i, 1), :] for i in range(4)], axis=1) >> 8
        et6[:, c] = split(jnp.concatenate([jnp.where(high == h, term, 0.0) for h in range(3)], axis=0), 2)

    grel = grel_q + join(mm(et6[...], ort[...], NT), 2)

    gmat[...] = jnp.zeros_like(gmat)
    gmat[:, 0:256] = grel[:dd]
    gmat[:, 256:512] = grel[dd : 2 * dd]
    gmat[:, 512:768] = grel[2 * dd :]
    gmat[:, 544 : 544 + dd] = glayer
    gmat[:, 576 : 576 + hid] = gent
    gmat[:, 640 : 640 + hid] = gquery
    gmat[0:1, 704 : 704 + hid] = gscore
    for c in range(6):
        for r in range(4):
            rsrc[c * 4 + r] = gmat[r * 8 : r * 8 + 8, c * 128 : (c + 1) * 128]

    own = me < TILES

    def send_tile(to):
        @pl.when(to < TILES)
        def _():
            pltpu.make_async_remote_copy(
                src_ref=rsrc.at[to],
                dst_ref=rsbuf.at[me],
                send_sem=r_send,
                recv_sem=r_recv,
                device_id=node_of(to),
                device_id_type=MESH,
            ).start()

    for to in peers():
        send_tile(to)

    def wait_for(ref, sem):
        pltpu.make_async_copy(ref, ref, sem).wait()

    @pl.when(own)
    def _():
        rsbuf[me] = rsrc[me]
        wait_for(rsbuf.at[pl.ds(0, nodes - 1)], r_recv)
        zbuf[mz] = jnp.sum(rsbuf[...], axis=0)

        @pl.loop(1, zs)
        def _(k):
            pltpu.make_async_remote_copy(
                src_ref=zbuf.at[mz],
                dst_ref=zbuf.at[mz],
                send_sem=z_send,
                recv_sem=z_recv,
                device_id=(me, (mz + k) % zs),
                device_id_type=MESH,
            ).start()

        if zs > 1:
            wait_for(zbuf.at[pl.ds(0, zs - 1)], z_recv)
        ag[me] = jnp.sum(zbuf[...], axis=0)

        for to in peers():
            pltpu.make_async_remote_copy(
                src_ref=ag.at[me],
                dst_ref=ag.at[me],
                send_sem=a_send,
                recv_sem=a_recv,
                device_id=node_of(to),
                device_id_type=MESH,
            ).start()

    new_out[...] = transposed(rows_of(new_all, nq, ent))

    wait_for(sbuf.at[chunk(0, nodes - 1)], s_send)
    wait_for(trecv.at[pl.ds(0, nodes - 1)], t_send)

    @pl.when(own)
    def _():
        wait_for(rsrc.at[pl.ds(0, TILES - 1)], r_send)
        if zs > 1:
            wait_for(zbuf.at[pl.ds(0, zs - 1)], z_send)
        wait_for(ag.at[pl.ds(0, TILES - 1)], a_recv)
        wait_for(rsbuf.at[pl.ds(0, nodes - 1)], a_send)

    @pl.when(jnp.logical_not(own))
    def _():
        wait_for(rsrc, r_send)
        wait_for(ag, a_recv)


def finish(
    new, loss, ag,
    new_o, loss_o, grel_o, glayer_o, gent_o, gquery_o, gscore_o,
    gmat, v_loss, v_rel, v_layer, v_ent, v_query, v_score, sem,
):
    first = pltpu.make_async_copy(new, new_o, sem.at[0])
    first.start()
    for c in range(6):
        for r in range(4):
            gmat[r * 8 : r * 8 + 8, c * 128 : (c + 1) * 128] = ag[c * 4 + r]
    nrel = v_rel.shape[1]
    dd, hid = v_ent.shape
    v_rel[...] = gmat[:, 0:nrel]
    copies = [pltpu.make_async_copy(v_rel, grel_o, sem.at[1])]
    v_layer[...] = gmat[:, 544 : 544 + dd]
    v_ent[...] = gmat[:, 576 : 576 + hid]
    v_query[...] = gmat[:, 640 : 640 + hid]
    v_score[...] = gmat[0:1, 704 : 704 + hid]
    v_loss[...] = loss[:, 0 : v_loss.shape[1]]
    pairs = ((v_layer, glayer_o), (v_ent, gent_o), (v_query, gquery_o), (v_score, gscore_o), (v_loss, loss_o))
    for i, (src, dst) in enumerate(pairs):
        copies.append(pltpu.make_async_copy(src, dst, sem.at[2 + i]))
    for copy in copies:
        copy.start()
    for copy in [first, *copies]:
        copy.wait()


def body(
    sizes,
    state_in, edge_src, edge_dst, edge_rel, edge_count, send_list, query_head, query_rel, pos_tail,
    neg_ids, rel_table, layer_weight, mlp_entity, mlp_query, score_weight,
):
    nodes, zs, nx, ny = sizes
    ent, width = state_in.shape
    nrel, dd = rel_table.shape
    hid = mlp_entity.shape[1]
    nq = width // dd
    edges = edge_src.shape[0]
    bnd = send_list.shape[2]
    sds = jax.ShapeDtypeStruct
    vmem = pl.BlockSpec(memory_space=pltpu.VMEM)
    hbm = pl.BlockSpec(memory_space=pltpu.HBM)
    dma = pltpu.SemaphoreType.DMA
    I32 = jnp.int32
    scratch = [
        pltpu.VMEM((ent, width), F32),
        pltpu.VMEM((ent + nodes * bnd, width), F32),
        pltpu.VMEM((nodes * bnd, width), F32),
        pltpu.VMEM((edges // 128, 128), I32),
        pltpu.VMEM((edges // 128, 128), I32),
        pltpu.VMEM(neg_ids.shape, I32),
        pltpu.VMEM((dd, nrel), F32),
        pltpu.VMEM((dd, dd), F32),
        pltpu.VMEM((dd, hid), F32),
        pltpu.VMEM((dd, hid), F32),
        pltpu.VMEM((1, hid), F32),
        pltpu.SMEM((edges,), I32),
        pltpu.SMEM((nodes, bnd), I32),
        pltpu.SMEM((1,), I32),
        pltpu.SMEM((nq,), I32),
        pltpu.SMEM((nq,), I32),
        pltpu.SMEM((nq,), I32),
        pltpu.VMEM((dd, 768), F32),
        pltpu.VMEM((9 * dd, 256), BF16),
        pltpu.VMEM((width, ent), F32),
        pltpu.VMEM((edges, width), F32),
        pltpu.VMEM((256, edges), BF16),
        pltpu.VMEM((ent, edges), BF16),
        pltpu.VMEM((edges, width), F32),
        pltpu.VMEM((width, edges), F32),
        pltpu.VMEM((edges, 3 * width), BF16),
        pltpu.VMEM((ent, 3 * width), F32),
        pltpu.VMEM((6 * dd, edges), BF16),
        pltpu.VMEM((1, 128), F32),
        pltpu.VMEM((nodes, 1, 128), F32),
        pltpu.VMEM((dd, 768), F32),
        pltpu.VMEM((TILES, 8, 128), F32),
        pltpu.VMEM((nodes, 8, 128), F32),
        pltpu.VMEM((zs, 8, 128), F32),
        dma((16,)), dma, dma, dma, dma, dma, dma, dma, dma, dma, dma,
    ]
    new, loss, ag = pl.pallas_call(
        functools.partial(kernel, (nodes, zs, nx, ny, nq * zs)),
        out_shape=(sds((ent, width), F32), sds((1, 128), F32), sds((TILES, 8, 128), F32)),
        in_specs=[hbm] * 15,
        out_specs=[vmem] * 3,
        scratch_shapes=scratch,
        compiler_params=pltpu.CompilerParams(
            collective_id=0, has_side_effects=True
        ),
        name="layer",
    )(
        state_in,
        edge_src,
        edge_dst.reshape(edges // 128, 128),
        edge_rel.reshape(edges // 128, 128),
        send_list.reshape(nodes, bnd),
        neg_ids,
        rel_table.T,
        layer_weight,
        mlp_entity,
        mlp_query,
        score_weight.reshape(1, hid),
        edge_count,
        query_head,
        query_rel,
        pos_tail,
    )
    shapes = [(1, nq), (dd, nrel), (dd, dd), (dd, hid), (dd, hid), (1, hid)]
    new_state, loss, grel, glayer, gent, gquery, gscore = pl.pallas_call(
        finish,
        out_shape=[sds((ent, width), F32)] + [sds(s, F32) for s in shapes],
        in_specs=[vmem] * 3,
        out_specs=[hbm] * 7,
        scratch_shapes=[pltpu.VMEM((dd, 768), F32)] + [pltpu.VMEM(s, F32) for s in shapes] + [dma((7,))],
        name="finish",
    )(new, loss, ag)
    return new_state, loss.reshape(nq), grel.T, glayer, gent, gquery, gscore.reshape(hid)


def solution(mesh):
    nodes, zs = mesh.shape["nodes"], mesh.shape["queries"]
    nx = 4
    ny = nodes // (2 * nx)
    in_specs = (
        P("nodes", "queries"),
        P("nodes"),
        P("nodes"),
        P("nodes"),
        P("nodes"),
        P("nodes", None, None),
        P("queries"),
        P("queries"),
        P("queries"),
        P("queries", "nodes"),
        P(),
        P(),
        P(),
        P(),
        P(),
    )
    out_specs = (P("nodes", "queries"), P("queries"), P(), P(), P(), P(), P())
    return jax.shard_map(
        functools.partial(body, (nodes, zs, nx, ny)),
        mesh=mesh, in_specs=in_specs, out_specs=out_specs, check_vma=False,
    )
```

```python
import functools

import jax
import jax.numpy as jnp
from jax import lax
from jax.experimental import pallas as pl
from jax.experimental.pallas import tpu as pltpu
from jax.sharding import PartitionSpec as P

adversarial = 0.5
MESH = pl.DeviceIdType.MESH
HIGH = lax.Precision.HIGHEST
F32 = jnp.float32
BF16 = jnp.bfloat16
NT = (((1,), (1,)), ((), ()))
NN = (((1,), (0,)), ((), ()))
TILES = 24
BLK = 256
WIDE = 1024


def mm(a, b, dims=NN, precision=None):
    return lax.dot_general(a, b, dims, precision=precision, preferred_element_type=F32)


def parts_of(x, terms):
    parts = []
    for i in range(terms):
        part = x.astype(BF16)
        parts.append(part)
        if i + 1 < terms:
            x = x - part.astype(F32)
    return parts


def split(x, terms, axis=0):
    return jnp.concatenate(parts_of(x, terms), axis=axis)


def join(y, terms):
    rows = y.shape[0] // terms
    out = y[:rows]
    for i in range(1, terms):
        out = out + y[i * rows : (i + 1) * rows]
    return out


def onehot(row, depth):
    ids = lax.broadcasted_iota(jnp.int32, (depth, row.shape[1]), 0)
    return jnp.where(ids == row, 1.0, 0.0).astype(BF16)


def lanes_of(x, queries, rows):
    return jnp.concatenate([x[q * rows : (q + 1) * rows] for q in range(queries)], axis=1)


def rows_of(x, queries, width):
    return jnp.concatenate([x[:, q * width : (q + 1) * width] for q in range(queries)], axis=0)


def transposed(x):
    r, c = x.shape
    return jnp.concatenate(
        [
            jnp.concatenate([x[i : i + 128, j : j + 128].T for i in range(0, r, 128)], axis=1)
            for j in range(0, c, 128)
        ],
        axis=0,
    )


def softplus(x):
    return jnp.maximum(x, 0.0) + jnp.log1p(jnp.exp(-jnp.abs(x)))


def sigmoid(x):
    return 1.0 / (1.0 + jnp.exp(-x))


def far_first(nx, ny):
    def away(d, n):
        return min(d, n - d)

    steps = [(dx, dy) for dy in range(ny) for dx in range(nx) if (dx, dy) != (0, 0)]
    return sorted(steps, key=lambda s: (-away(s[0], nx) - away(s[1], ny), s))


def kernel(
    cfg,
    h_state, h_esrc, h_edst, h_erel, h_slist, h_neg, h_rel, h_wl, h_me, h_mq, h_sw,
    h_count, h_head, h_qrel, h_tail,
    new_out, loss_out, ag,
    st_v, tab, sbuf, edst, erel, neg, relraw, wl, me_w, mq_w, sw,
    esrc, slist, ecount, qhead, qrel, ptail,
    relpad, rt9, stt_ref, relrow, ort, odt, srcr, srct, msg3, acc, et6,
    tsend, trecv, gmat, rsrc, rsbuf, zbuf,
    i_sem, s_send, s_recv, t_send, t_recv, r_send, r_recv, z_send, z_recv, a_send, a_recv,
):
    nodes, zs, nx, ny, queries_total = cfg
    me = lax.axis_index("nodes")
    mz = lax.axis_index("queries")
    chip = me // 2
    core = me % 2
    cx = chip % nx
    cy = chip // nx
    dd, hid = me_w.shape
    ent = h_state.shape[0]
    nq = h_state.shape[1] // dd
    edges = h_esrc.shape[0]
    bnd = h_slist.shape[1]
    blocks = edges // BLK
    nrel = relraw.shape[1]
    lane128 = lax.broadcasted_iota(jnp.int32, (1, 128), 1)

    def node_of(t):
        return (t, mz)

    loads = [
        pltpu.make_async_copy(src, dst, i_sem.at[i])
        for i, (src, dst) in enumerate(
            (
                (h_slist, slist), (h_state, st_v), (h_state, tab.at[pl.ds(0, ent)]), (h_rel, relraw), (h_erel, erel),
                (h_edst, edst), (h_esrc, esrc), (h_count, ecount), (h_qrel, qrel), (h_head, qhead),
                (h_tail, ptail), (h_neg, neg), (h_wl, wl), (h_me, me_w), (h_mq, mq_w), (h_sw, sw),
            )
        )
    ]
    for load in loads:
        load.start()
    barrier = pltpu.get_barrier_semaphore()

    def peers():
        for dx, dy in far_first(nx, ny):
            there = 2 * (((cy + dy) % ny) * nx + (cx + dx) % nx)
            yield there + core
            yield there + 1 - core
        yield 2 * chip + 1 - core

    for to in peers():
        pl.semaphore_signal(barrier, inc=1, device_id=node_of(to), device_id_type=MESH)
    for k in range(1, zs):
        pl.semaphore_signal(barrier, inc=1, device_id=(me, (mz + k) % zs), device_id_type=MESH)

    loads[0].wait()
    loads[1].wait()

    for b in range(nodes):
        for k in range(bnd):
            e = b * bnd + k
            sbuf[e : e + 1, :] = st_v[pl.ds(slist[b, k], 1), :]

    pl.semaphore_wait(barrier, nodes - 1 + zs - 1)

    def chunk(first, n=1):
        return pl.ds(pl.multiple_of(first * bnd, bnd), n * bnd)

    def send_rows(to):
        pltpu.make_async_remote_copy(
            src_ref=sbuf.at[chunk(to)],
            dst_ref=tab.at[pl.ds(pl.multiple_of(ent + me * bnd, bnd), bnd)],
            send_sem=s_send,
            recv_sem=s_recv,
            device_id=node_of(to),
            device_id_type=MESH,
        ).start()

    for to in peers():
        send_rows(to)
    tab[pl.ds(pl.multiple_of(ent + me * bnd, bnd), bnd), :] = sbuf[chunk(me), :]

    for load in loads[2:]:
        load.wait()
    stt_ref[...] = transposed(st_v[...])
    relpad[...] = jnp.zeros_like(relpad)
    relpad[:, 0:nrel] = relraw[...]
    rt9[...] = jnp.concatenate([split(relpad[:, h * 256 : (h + 1) * 256], 3) for h in range(3)], axis=0)

    def edge_row(ref, j):
        return jnp.concatenate([ref[pl.ds(2 * j, 1), :], ref[pl.ds(2 * j + 1, 1), :]], axis=1)

    def at_block(j, size=BLK):
        if isinstance(j, int):
            return slice(j * size, (j + 1) * size)
        return pl.ds(pl.multiple_of(j * size, size), size)

    def relation(hot, high):
        got = mm(rt9[...], hot)
        out = jnp.zeros((dd, hot.shape[1]), F32)
        for h in range(3):
            out = jnp.where(high == h, join(got[h * 3 * dd : (h + 1) * 3 * dd], 3), out)
        return out

    lane256 = lax.broadcasted_iota(jnp.int32, (1, BLK), 1)

    @pl.loop(0, blocks)
    def _(j):
        row = edge_row(erel, j)
        hot = onehot(row & 255, 256)
        ort[:, at_block(j)] = hot
        relrow[at_block(j), :] = transposed(jnp.concatenate([relation(hot, row >> 8)] * nq, axis=0))
        dst = jnp.where(lane256 + j * BLK < ecount[0], edge_row(edst, j), -1)
        odt[:, at_block(j)] = onehot(dst, ent)

    qr = jnp.full((1, 128), -1, jnp.int32)
    for q in range(nq):
        qr = jnp.where(lane128 == q, qrel[q], qr)
    q_hot = onehot(qr & 255, 256)
    q_high = qr >> 8
    qvt = relation(q_hot, q_high)
    lane_ent = lax.broadcasted_iota(jnp.int32, (1, ent), 1)

    def local_of(g):
        return jnp.where(g // ent == me, g % ent, -1)

    heads = [jnp.where(lane_ent == local_of(qhead[q]), 1.0, 0.0) for q in range(nq)]
    tails = [jnp.where(lane_ent == local_of(ptail[q]), 1.0, 0.0) for q in range(nq)]
    head_term = jnp.concatenate([qvt[:, q : q + 1] * heads[q] for q in range(nq)], axis=1)
    qh = mm(mq_w[...].T, qvt, precision=HIGH)
    qh_wide = jnp.concatenate(
        [jnp.broadcast_to(qh[:, q : q + 1], (hid, 128)) for q in range(nq)] + [qh], axis=1
    )
    eye = lax.broadcasted_iota(jnp.int32, (hid, hid), 0) == lax.broadcasted_iota(jnp.int32, (hid, hid), 1)
    swc = jnp.sum(jnp.where(eye, sw[...], 0.0), axis=1, keepdims=True)
    acc[...] = jnp.zeros_like(acc)

    pltpu.make_async_copy(sbuf.at[chunk(0, nodes - 1)], sbuf.at[chunk(0, nodes - 1)], s_recv).wait()

    def gather(j):
        for u in range(BLK):
            e = j * BLK + u
            srcr[pl.ds(e, 1), :] = tab[pl.ds(esrc[e], 1), :]
        msg3[at_block(j), :] = split(srcr[at_block(j), :] * relrow[at_block(j), :], 3, axis=1)

    def scatter(j):
        acc[...] += mm(odt[:, at_block(j)], msg3[at_block(j), :])

    gather(0)

    @pl.loop(0, (blocks - 1) // 5)
    def _(t):
        for i in range(5):
            scatter(5 * t + i)
            gather(5 * t + i + 1)

    scatter(blocks - 1)
    width = nq * dd
    summed = acc[:, 0:width] + acc[:, width : 2 * width] + acc[:, 2 * width : 3 * width]
    s_all = lanes_of(transposed(summed), nq, dd) + head_term
    pre = mm(wl[...].T, s_all, precision=HIGH)
    new_all = lanes_of(stt_ref[...], nq, dd) + jnp.maximum(pre, 0.0)

    picks = []
    hots = []
    pos_pick = jnp.zeros((dd, 128), F32)
    is_pos = lane128 < 0
    for q in range(nq):
        mine = new_all[:, q * ent : (q + 1) * ent]
        ids = neg[q : q + 1, :]
        low = jnp.broadcast_to(ids & 127, (dd, 128))
        out = jnp.zeros((dd, 128), F32)
        for b in range(ent // 128):
            got = jnp.take_along_axis(
                mine[:, b * 128 : (b + 1) * 128], low, axis=1, mode="promise_in_bounds"
            )
            out = jnp.where((ids >> 7) == b, got, out)
        picks.append(out)
        hots.append(onehot(ids, ent))
        pos_pick = jnp.where(lane128 == q, jnp.sum(mine * tails[q], axis=1, keepdims=True), pos_pick)
        is_pos = is_pos | ((lane128 == q) & (ptail[q] // ent == me))
    picked = jnp.concatenate(picks + [pos_pick], axis=1)
    pre_h = mm(me_w[...].T, picked, precision=HIGH) + qh_wide
    act = jnp.maximum(pre_h, 0.0)
    score = jnp.sum(act * swc, axis=0, keepdims=True)
    nneg = nq * 128
    s_neg = rows_of(score[:, :nneg], nq, 128)
    s_pos = score[:, nneg:]
    weight = jnp.exp(adversarial * s_neg)
    part_total = jnp.sum(weight, axis=1, keepdims=True)
    part_weighted = jnp.sum(weight * softplus(s_neg), axis=1, keepdims=True)
    sub = lax.broadcasted_iota(jnp.int32, (nq, 128), 0)
    lanes = lax.broadcasted_iota(jnp.int32, (nq, 128), 1)

    def row_of(col, first):
        return jnp.sum(jnp.where(lanes == sub + first, col, 0.0), axis=0, keepdims=True)

    part_row = row_of(part_total, 0)
    pos_terms = jnp.where(is_pos, softplus(-s_pos), 0.0)
    line = part_row + row_of(part_weighted, nq) + pltpu.roll(pos_terms, 2 * nq, 1)
    tsend[...] = line
    trecv[me] = line
    for to in peers():
        pltpu.make_async_remote_copy(
            src_ref=tsend,
            dst_ref=trecv.at[me],
            send_sem=t_send,
            recv_sem=t_recv,
            device_id=node_of(to),
            device_id_type=MESH,
        ).start()

    safe = jnp.where(part_total > 0, part_total, 1.0)
    c_neg = weight / safe * sigmoid(s_neg) / queries_total
    c_pos = jnp.where(is_pos, sigmoid(s_pos) - 1.0, 0.0) / queries_total
    coef = jnp.concatenate([c_neg[q : q + 1] for q in range(nq)] + [c_pos], axis=1)
    gh = coef * swc * jnp.where(pre_h > 0, 1.0, 0.0)
    gp = mm(me_w[...], gh, precision=HIGH)
    gc_neg = jnp.concatenate(
        [join(mm(split(gp[:, q * 128 : (q + 1) * 128], 3), hots[q], NT), 3) for q in range(nq)], axis=1
    )
    gc_pos = jnp.concatenate([gp[:, nneg + q : nneg + q + 1] * tails[q] for q in range(nq)], axis=1)
    gpre = jnp.concatenate([jnp.where(pre > 0, gc_neg, 0.0), jnp.where(pre > 0, gc_pos, 0.0)], axis=1)
    gsum = mm(wl[...], gpre, precision=HIGH)
    half = nq * ent
    gs_neg = rows_of(gsum[:, :half], nq, ent)
    gs_pos = rows_of(gsum[:, half:], nq, ent)

    ht_neg = jnp.zeros((hid, 128), F32)
    hd_neg = jnp.zeros((dd, 128), F32)
    hd_pos = jnp.zeros((dd, 128), F32)
    scores8 = jnp.broadcast_to(coef, (8, nneg + 128))
    ent_q, lay_q, sco_q = [], [], []
    lay_pos = jnp.zeros((dd, dd), F32)
    for q in range(nq):
        tile = slice(q * 128, (q + 1) * 128)
        cols = slice(q * ent, (q + 1) * ent)
        here = lane128 == q
        ht_neg = jnp.where(here, jnp.sum(gh[:, tile], axis=1, keepdims=True), ht_neg)
        hd_neg = jnp.where(here, jnp.sum(gsum[:, cols] * heads[q], axis=1, keepdims=True), hd_neg)
        g_p = gsum[:, half + q * ent : half + (q + 1) * ent]
        hd_pos = jnp.where(here, jnp.sum(g_p * heads[q], axis=1, keepdims=True), hd_pos)
        ent_q.append(mm(picked[:, tile], gh[:, tile], NT, HIGH))
        sco_q.append(mm(scores8[:, tile], act[:, tile], NT, HIGH)[0:1])
        lay_q.append(mm(s_all[:, cols], gpre[:, cols], NT, HIGH))
    lay_pos = mm(s_all, gpre[:, half:], NT, HIGH)
    ent_pos = mm(pos_pick, gh[:, nneg:], NT, HIGH)
    sco_pos = mm(scores8[:, nneg:], act[:, nneg:], NT, HIGH)[0:1]

    @pl.loop(0, edges // BLK)
    def _(j):
        srct[:, at_block(j)] = transposed(srcr[at_block(j), :])

    pltpu.make_async_copy(trecv.at[pl.ds(0, nodes - 1)], trecv.at[pl.ds(0, nodes - 1)], t_recv).wait()
    totals = jnp.sum(trecv[...], axis=0)
    loss_out[...] = pltpu.roll(totals, 128 - 2 * nq, 1) + pltpu.roll(totals, 128 - nq, 1) / totals
    ratio = jnp.where(lane128 < nq, part_row / totals, 0.0)
    ratios = [ratio[:, q : q + 1] for q in range(nq)]
    gs = jnp.concatenate([gs_neg[q * dd : (q + 1) * dd] * ratios[q] for q in range(nq)], axis=0) + gs_pos
    gs2 = split(gs, 2)

    ht = ht_neg * ratio + gh[:, nneg:]
    gq = mm(mq_w[...], ht, precision=HIGH) + hd_neg * ratio + hd_pos
    gquery = mm(qvt, ht, NT, HIGH)
    gent = ent_pos + sum(ent_q[q] * ratios[q] for q in range(nq))
    glayer = lay_pos + sum(lay_q[q] * ratios[q] for q in range(nq))
    gscore = sco_pos + sum(sco_q[q] * ratios[q] for q in range(nq))
    gq9 = split(jnp.concatenate([jnp.where(q_high == h, gq, 0.0) for h in range(3)], axis=0), 3)
    grel_q = join(mm(gq9, q_hot, NT), 3)

    @pl.loop(0, edges // WIDE)
    def _(j):
        c = at_block(j, WIDE)
        up = join(mm(gs2, odt[:, c]), 2) * srct[:, c]
        term = join(up, nq)
        high = jnp.concatenate([erel[pl.ds(WIDE // 128 * j + i, 1), :] for i in range(WIDE // 128)], axis=1) >> 8
        et6[:, c] = split(jnp.concatenate([jnp.where(high == h, term, 0.0) for h in range(3)], axis=0), 2)

    grel = grel_q + join(mm(et6[...], ort[...], NT), 2)

    gmat[...] = jnp.zeros_like(gmat)
    gmat[:, 0:256] = grel[:dd]
    gmat[:, 256:512] = grel[dd : 2 * dd]
    gmat[:, 512:768] = grel[2 * dd :]
    gmat[:, 544 : 544 + dd] = glayer
    gmat[:, 576 : 576 + hid] = gent
    gmat[:, 640 : 640 + hid] = gquery
    gmat[0:1, 704 : 704 + hid] = gscore
    for c in range(6):
        for r in range(4):
            rsrc[c * 4 + r] = gmat[r * 8 : r * 8 + 8, c * 128 : (c + 1) * 128]

    own = me < TILES

    def send_tile(to):
        @pl.when(to < TILES)
        def _():
            pltpu.make_async_remote_copy(
                src_ref=rsrc.at[to],
                dst_ref=rsbuf.at[me],
                send_sem=r_send,
                recv_sem=r_recv,
                device_id=node_of(to),
                device_id_type=MESH,
            ).start()

    for to in peers():
        send_tile(to)

    def wait_for(ref, sem):
        pltpu.make_async_copy(ref, ref, sem).wait()

    @pl.when(own)
    def _():
        rsbuf[me] = rsrc[me]
        wait_for(rsbuf.at[pl.ds(0, nodes - 1)], r_recv)
        zbuf[mz] = jnp.sum(rsbuf[...], axis=0)

        @pl.loop(1, zs)
        def _(k):
            pltpu.make_async_remote_copy(
                src_ref=zbuf.at[mz],
                dst_ref=zbuf.at[mz],
                send_sem=z_send,
                recv_sem=z_recv,
                device_id=(me, (mz + k) % zs),
                device_id_type=MESH,
            ).start()

        if zs > 1:
            wait_for(zbuf.at[pl.ds(0, zs - 1)], z_recv)
        ag[me] = jnp.sum(zbuf[...], axis=0)

        for to in peers():
            pltpu.make_async_remote_copy(
                src_ref=ag.at[me],
                dst_ref=ag.at[me],
                send_sem=a_send,
                recv_sem=a_recv,
                device_id=node_of(to),
                device_id_type=MESH,
            ).start()

    new_out[...] = transposed(rows_of(new_all, nq, ent))

    wait_for(sbuf.at[chunk(0, nodes - 1)], s_send)
    wait_for(trecv.at[pl.ds(0, nodes - 1)], t_send)

    @pl.when(own)
    def _():
        wait_for(rsrc.at[pl.ds(0, TILES - 1)], r_send)
        if zs > 1:
            wait_for(zbuf.at[pl.ds(0, zs - 1)], z_send)
        wait_for(ag.at[pl.ds(0, TILES - 1)], a_recv)
        wait_for(rsbuf.at[pl.ds(0, nodes - 1)], a_send)

    @pl.when(jnp.logical_not(own))
    def _():
        wait_for(rsrc, r_send)
        wait_for(ag, a_recv)


def finish(
    new, loss, ag,
    new_o, loss_o, grel_o, glayer_o, gent_o, gquery_o, gscore_o,
    gmat, v_loss, v_rel, v_layer, v_ent, v_query, v_score, sem,
):
    first = pltpu.make_async_copy(new, new_o, sem.at[0])
    first.start()
    for c in range(6):
        for r in range(4):
            gmat[r * 8 : r * 8 + 8, c * 128 : (c + 1) * 128] = ag[c * 4 + r]
    nrel = v_rel.shape[1]
    dd, hid = v_ent.shape
    v_rel[...] = gmat[:, 0:nrel]
    copies = [pltpu.make_async_copy(v_rel, grel_o, sem.at[1])]
    v_layer[...] = gmat[:, 544 : 544 + dd]
    v_ent[...] = gmat[:, 576 : 576 + hid]
    v_query[...] = gmat[:, 640 : 640 + hid]
    v_score[...] = gmat[0:1, 704 : 704 + hid]
    v_loss[...] = loss[:, 0 : v_loss.shape[1]]
    pairs = ((v_layer, glayer_o), (v_ent, gent_o), (v_query, gquery_o), (v_score, gscore_o), (v_loss, loss_o))
    for i, (src, dst) in enumerate(pairs):
        copies.append(pltpu.make_async_copy(src, dst, sem.at[2 + i]))
    for copy in copies:
        copy.start()
    for copy in [first, *copies]:
        copy.wait()


def body(
    sizes,
    state_in, edge_src, edge_dst, edge_rel, edge_count, send_list, query_head, query_rel, pos_tail,
    neg_ids, rel_table, layer_weight, mlp_entity, mlp_query, score_weight,
):
    nodes, zs, nx, ny = sizes
    ent, width = state_in.shape
    nrel, dd = rel_table.shape
    hid = mlp_entity.shape[1]
    nq = width // dd
    edges = edge_src.shape[0]
    bnd = send_list.shape[2]
    sds = jax.ShapeDtypeStruct
    vmem = pl.BlockSpec(memory_space=pltpu.VMEM)
    hbm = pl.BlockSpec(memory_space=pltpu.HBM)
    dma = pltpu.SemaphoreType.DMA
    I32 = jnp.int32
    scratch = [
        pltpu.VMEM((ent, width), F32),
        pltpu.VMEM((ent + nodes * bnd, width), F32),
        pltpu.VMEM((nodes * bnd, width), F32),
        pltpu.VMEM((edges // 128, 128), I32),
        pltpu.VMEM((edges // 128, 128), I32),
        pltpu.VMEM(neg_ids.shape, I32),
        pltpu.VMEM((dd, nrel), F32),
        pltpu.VMEM((dd, dd), F32),
        pltpu.VMEM((dd, hid), F32),
        pltpu.VMEM((dd, hid), F32),
        pltpu.VMEM((1, hid), F32),
        pltpu.SMEM((edges,), I32),
        pltpu.SMEM((nodes, bnd), I32),
        pltpu.SMEM((1,), I32),
        pltpu.SMEM((nq,), I32),
        pltpu.SMEM((nq,), I32),
        pltpu.SMEM((nq,), I32),
        pltpu.VMEM((dd, 768), F32),
        pltpu.VMEM((9 * dd, 256), BF16),
        pltpu.VMEM((width, ent), F32),
        pltpu.VMEM((edges, width), F32),
        pltpu.VMEM((256, edges), BF16),
        pltpu.VMEM((ent, edges), BF16),
        pltpu.VMEM((edges, width), F32),
        pltpu.VMEM((width, edges), F32),
        pltpu.VMEM((edges, 3 * width), BF16),
        pltpu.VMEM((ent, 3 * width), F32),
        pltpu.VMEM((6 * dd, edges), BF16),
        pltpu.VMEM((1, 128), F32),
        pltpu.VMEM((nodes, 1, 128), F32),
        pltpu.VMEM((dd, 768), F32),
        pltpu.VMEM((TILES, 8, 128), F32),
        pltpu.VMEM((nodes, 8, 128), F32),
        pltpu.VMEM((zs, 8, 128), F32),
        dma((16,)), dma, dma, dma, dma, dma, dma, dma, dma, dma, dma,
    ]
    new, loss, ag = pl.pallas_call(
        functools.partial(kernel, (nodes, zs, nx, ny, nq * zs)),
        out_shape=(sds((ent, width), F32), sds((1, 128), F32), sds((TILES, 8, 128), F32)),
        in_specs=[hbm] * 15,
        out_specs=[vmem] * 3,
        scratch_shapes=scratch,
        compiler_params=pltpu.CompilerParams(
            collective_id=0, has_side_effects=True
        ),
        name="layer",
    )(
        state_in,
        edge_src,
        edge_dst.reshape(edges // 128, 128),
        edge_rel.reshape(edges // 128, 128),
        send_list.reshape(nodes, bnd),
        neg_ids,
        rel_table.T,
        layer_weight,
        mlp_entity,
        mlp_query,
        score_weight.reshape(1, hid),
        edge_count,
        query_head,
        query_rel,
        pos_tail,
    )
    shapes = [(1, nq), (dd, nrel), (dd, dd), (dd, hid), (dd, hid), (1, hid)]
    new_state, loss, grel, glayer, gent, gquery, gscore = pl.pallas_call(
        finish,
        out_shape=[sds((ent, width), F32)] + [sds(s, F32) for s in shapes],
        in_specs=[vmem] * 3,
        out_specs=[hbm] * 7,
        scratch_shapes=[pltpu.VMEM((dd, 768), F32)] + [pltpu.VMEM(s, F32) for s in shapes] + [dma((7,))],
        name="finish",
    )(new, loss, ag)
    return new_state, loss.reshape(nq), grel.T, glayer, gent, gquery, gscore.reshape(hid)


def solution(mesh):
    nodes, zs = mesh.shape["nodes"], mesh.shape["queries"]
    nx = 4
    ny = nodes // (2 * nx)
    in_specs = (
        P("nodes", "queries"),
        P("nodes"),
        P("nodes"),
        P("nodes"),
        P("nodes"),
        P("nodes", None, None),
        P("queries"),
        P("queries"),
        P("queries"),
        P("queries", "nodes"),
        P(),
        P(),
        P(),
        P(),
        P(),
    )
    out_specs = (P("nodes", "queries"), P("queries"), P(), P(), P(), P(), P())
    return jax.shard_map(
        functools.partial(body, (nodes, zs, nx, ny)),
        mesh=mesh, in_specs=in_specs, out_specs=out_specs, check_vma=False,
    )
```
